32 devices in a mesh: grp: 2 (over x), slab: 16 (over z, y, core).
Axes of the slice: x: 2, y: 2, z: 4, core: 2. Of those that a mesh axis runs over, the one named last changes fastest.
Arguments:
- activations: bfloat16 [32, 96, 1024], P(('grp', 'slab')), parts along dimension 0, may hold values from -6 to 6
- weights: bfloat16 [3, 3, 3, 192, 192], replicated, may hold values from -0.078125 to 0.078125
- cotangent: bfloat16 [32, 96, 1024], P(('grp', 'slab')), parts along dimension 0, may hold values from -6 to 6
Outputs:
- forward: bfloat16 [32, 96, 1024], P(('grp', 'slab')), parts along dimension 0
- input_grad: bfloat16 [32, 96, 1024], P(('grp', 'slab')), parts along dimension 0
- weight_grad: float32 [32, 62208], P(('grp', 'slab')), parts along dimension 0
The draws below stay inside these ranges and needn't reach their ends.
There are 2 independent parts, one for each index of `grp`. The reference program is written for one: setup_inputs(seed, part) draws one part's arguments, and reference() takes and returns one part's arrays. A program takes and returns all parts, laid end to end along the dimension named above; an argument that names none is the same for every part. Nothing has to cross between parts.
All inputs are finite; a program needn't handle non-finite values.
Results may differ from the reference program's by a relative error of at most 0.001.
Values may be sent and summed in bfloat16 or wider, within the bound.
No kernel may reach another device: no remote copies, remote signals or barrier semaphores. Data moves between devices by JAX's collectives and lax.ppermute only.
A program may use at most 128 MiB of HBM per device.

```python
import math
import jax
import jax.numpy as jnp
from jax import lax

CIN = 192
COUT = 192
KK = 27
H = 16
W = 64
NZ = 8
N_SLAB = 16


def levels(stream_key, shape, split, smallest, largest):
    level, own = 1.0, jax.random.fold_in(stream_key, 6)
    for dim, blocks in split:
        heights = jnp.exp(jax.random.uniform(jax.random.fold_in(own, dim), (blocks,), jnp.float32, smallest / len(split), largest / len(split)))
        level = level * jnp.repeat(heights, shape[dim] // blocks).reshape([-1 if axis == dim else 1 for axis in range(len(shape))])
    return level


def bell_draw(stream_key, extent, width, limit, shards=(), held_as=jnp.bfloat16):
    level = levels(stream_key, extent, shards, -0.22, 0.18) if shards else 1.0
    values = jax.random.normal(stream_key, extent, jnp.float32) * width * level
    return jnp.minimum(jnp.maximum(values, -limit), limit).astype(held_as)


def setup_inputs(seed: int = 0, part: int = 0) -> dict:
    key_list = jax.random.split(jax.random.key(seed), 4)
    part_keys = jax.random.split(jax.random.fold_in(key_list[3], part), 4)
    return {
        "activations": bell_draw(part_keys[0], (2 * NZ, CIN // 2, H * W), 1.0, 6.0, ((0, 16),)),
        "weights": bell_draw(key_list[1], (3, 3, 3, CIN, COUT), (KK * CIN) ** -0.5, 0.078125),
        "cotangent": bell_draw(part_keys[2], (2 * NZ, COUT // 2, H * W), 1.0, 6.0, ((0, 16),)),
    }


def to_volume(field, chans):
    return field.astype(jnp.float32).reshape(NZ, chans, H, W).transpose(1, 0, 2, 3)[None]

def from_volume(field, chans):
    return field[0].transpose(1, 0, 2, 3).reshape(2 * NZ, chans // 2, H * W)

def convolve(volume, kernel):
    return lax.conv_general_dilated(volume, kernel, (1, 1, 1), [(1, 1), (1, 1), (1, 1)], dimension_numbers=('NCDHW', 'DHWIO', 'NCDHW'), precision=lax.Precision.HIGHEST)

def reference(activations, weights, cotangent):
    volume = to_volume(activations, CIN)
    kernel = weights.astype(jnp.float32)
    result, pullback = jax.vjp(convolve, volume, kernel)
    back_volume, kernel_grad = pullback(to_volume(cotangent, COUT))
    forward = from_volume(result, COUT).astype(jnp.bfloat16)
    input_grad = from_volume(back_volume, CIN).astype(jnp.bfloat16)
    scaled = kernel_grad * (1.0 / math.sqrt(NZ * H * W))
    arranged = scaled.reshape(3, 3, 3, 2, CIN // 2, COUT).transpose(3, 0, 1, 2, 4, 5)
    return (forward, input_grad, arranged.reshape(N_SLAB, KK * CIN * COUT // N_SLAB))
```

```python
import functools
import math

import jax
import jax.numpy as jnp
from jax import lax
from jax.experimental import pallas as pl
from jax.experimental.pallas import tpu as pltpu
from jax.sharding import PartitionSpec as P

W = 64
AXIS = "slab"
F32 = jnp.float32
BF16 = jnp.bfloat16
TOP = 60000.0
IN_VMEM = pl.BlockSpec(memory_space=pltpu.VMEM)


def swapped(value, bit):
    count = lax.axis_size(AXIS)
    return lax.ppermute(value, AXIS, [(i, i ^ bit) for i in range(count)])


def relayed(value):
    count = lax.axis_size(AXIS)
    route = [(i, i - 4 if i & 2 else i + 4) for i in range(count)]
    return lax.ppermute(value, AXIS, [(i, j) for i, j in route if 0 <= j < count])


def place():
    index = lax.axis_index(AXIS)
    return index % 2, (index // 2) % 2, index % 4, index // 4


def call(body, outs, operands, scratch, flops, name):
    moved = sum(math.prod(a.shape) * a.dtype.itemsize for a in [*outs, *operands])
    return pl.pallas_call(
        body,
        out_shape=outs,
        in_specs=[IN_VMEM] * len(operands),
        out_specs=[IN_VMEM] * len(outs),
        scratch_shapes=scratch,
        cost_estimate=pl.CostEstimate(flops=flops, transcendentals=0, bytes_accessed=moved),
        compiler_params=pltpu.CompilerParams(vmem_limit_bytes=48 << 20),
        name=name,
    )(*operands)


def weight_body(w_ref, fwd_ref, back_ref):
    half, _, _, _ = place()
    chans, filters = w_ref.shape[3:]
    in_half, out_half = chans // 2, filters // 2
    start = pl.multiple_of(half * in_half, 32)
    for b in range(3):
        for e in range(3):
            block = 3 * b + e
            for a in range(3):
                turned = w_ref[a, b, e].T
                own = jnp.where(half == 0, turned[:out_half], turned[out_half:])
                fwd_ref[block * out_half : (block + 1) * out_half, a * chans : (a + 1) * chans] = own
                rows = w_ref[2 - a, 2 - b, 2 - e, pl.ds(start, in_half), :]
                back_ref[block * in_half : (block + 1) * in_half, a * filters : (a + 1) * filters] = rows


def weight_tables(weights):
    chans, filters = weights.shape[3:]
    outs = [
        jax.ShapeDtypeStruct((9 * filters // 2, 3 * chans), BF16),
        jax.ShapeDtypeStruct((9 * chans // 2, 3 * filters), BF16),
    ]
    return call(weight_body, outs, [weights], [], 0, "tables")


def fill(target, parts, half, first_row):
    rows = parts[0].shape[1]
    for part, which in zip(parts, (half, 1 - half)):
        target[pl.ds(pl.multiple_of(first_row + which * rows, 32), rows), :] = part[0]


def fold(product, out_ref, rows):
    size = product.shape[1]
    cell = lax.broadcasted_iota(jnp.int32, (rows, size), 1)
    column = cell % W

    def tap(b, e):
        block = 3 * b + e
        return product[block * rows : (block + 1) * rows, :]

    def over_rows(e):
        up = jnp.where(cell >= W, pltpu.roll(tap(0, e), W, 1), 0.0)
        down = jnp.where(cell < size - W, pltpu.roll(tap(2, e), size - W, 1), 0.0)
        return tap(1, e) + up + down

    left = jnp.where(column >= 1, pltpu.roll(over_rows(0), 1, 1), 0.0)
    right = jnp.where(column < W - 1, pltpu.roll(over_rows(2), size - 1, 1), 0.0)
    out_ref[0] = (over_rows(1) + left + right).astype(out_ref.dtype)


def conv_body(*refs):
    xs, ys = refs[0:6], refs[6:12]
    fwd_w, back_w, fwd_ref, back_ref, planes, product = refs[12:]
    half, odd, _, _ = place()
    for parts, table, out_ref in ((xs, fwd_w, fwd_ref), (ys, back_w, back_ref)):
        chans = 2 * parts[0].shape[1]
        for k, slot in enumerate((1, 2 - 2 * odd, 2 * odd)):
            fill(planes, parts[2 * k : 2 * k + 2], half, slot * chans)
        product[...] = jnp.dot(table[...], planes[...], preferred_element_type=F32)
        fold(product, out_ref, out_ref.shape[1])


def convolutions(xs, ys, tables):
    _, in_half, size = xs[0].shape
    out_half = ys[0].shape[1]
    outs = [
        jax.ShapeDtypeStruct((1, out_half, size), BF16),
        jax.ShapeDtypeStruct((1, in_half, size), BF16),
    ]
    scratch = [pltpu.VMEM((6 * in_half, size), BF16), pltpu.VMEM((9 * out_half, size), F32)]
    flops = 2 * 2 * 54 * in_half * out_half * size
    return call(conv_body, outs, [*xs, *ys, *tables], scratch, flops, "convolve")


def pieces(chunk, chunks, in_half):
    rows = 27 * in_half // chunks
    at, end, found = chunk * rows, (chunk + 1) * rows, []
    while at < end:
        tap, first = divmod(at, in_half)
        count = min(in_half - first, end - at)
        found.append((tap, first, count, at - chunk * rows))
        at += count
    return found


def moved(plane, b, e, cells):
    size = plane.shape[1]
    step = W * (b - 1) + e - 1
    if step:
        plane = pltpu.roll(plane, -step % size, 1)
    keep = None
    if b == 0:
        keep = cells >= W
    if b == 2:
        keep = cells < size - W
    if e != 1:
        inside = cells % W >= 1 if e == 0 else cells % W < W - 1
        keep = inside if keep is None else keep & inside
    return plane if keep is None else plane * keep.astype(F32).astype(plane.dtype)


def products(place4, pairs_of, accumulate, lhs, low, high, in_half):
    chunks = 8
    for a in range(3):
        pairs = pairs_of(a)
        rows = []
        for r in range(2):
            for tap, first, count, row in pieces(place4 + 4 * r, chunks, in_half):
                if tap // 9 == a:
                    begin, end = first // 16 * 16, -(-(first + count) // 16) * 16
                    rows.append((r, tap, first, count, row, begin, end))
        if not rows or not pairs:
            continue
        total = None
        for x_ref, y_ref in pairs:
            size = x_ref.shape[1]
            cells = lax.broadcasted_iota(jnp.int32, (1, size), 1)
            at = 0
            for r, tap, first, count, row, begin, end in rows:
                b, e = tap // 3 % 3, tap % 3
                for half in range(2):
                    source = x_ref[half * in_half + begin : half * in_half + end, :]
                    lhs[at : at + end - begin, :] = moved(source, b, e, cells)
                    at += end - begin
            term = lax.dot_general(
                lhs[0:at, :], y_ref[...], (((1,), (1,)), ((), ())), preferred_element_type=F32
            )
            total = term if total is None else total + term
        at = 0
        for r, tap, first, count, row, begin, end in rows:
            for half in range(2):
                got = total[at + first - begin : at + first - begin + count]
                at += end - begin
                chunk = 2 * half + r
                where = slice(row, row + count)
                if accumulate:
                    low[chunk, where, :] += got[:, :128]
                    high[chunk, where, 0:64] += got[:, 128:]
                else:
                    low[chunk, where, :] = got[:, :128]
                    high[chunk, where, 0:64] = got[:, 128:]


def largest(*refs):
    top = None
    for ref in refs:
        here = jnp.max(jnp.abs(ref[...].astype(F32)), axis=0, keepdims=True)
        top = here if top is None else jnp.maximum(top, here)
    return top


def near_body(xo, xop, xs, xsp, yo, yop, ys, ysp, low, high, top_x, top_y, xof, xsf, yof, ysf, lhs):
    half, _, mine, _ = place()
    in_half = xo.shape[1]
    for full, parts in ((xof, (xo, xop)), (xsf, (xs, xsp)), (yof, (yo, yop)), (ysf, (ys, ysp))):
        fill(full, parts, half, 0)
    high[...] = jnp.zeros_like(high)
    for place4 in range(4):
        lower, upper = ((xof, yof), (xsf, ysf)) if place4 < 2 else ((xsf, ysf), (xof, yof))

        def pairs_of(a, lower=lower, upper=upper):
            return ([(lower[0], upper[1])], [lower, upper], [(upper[0], lower[1])])[a]

        @pl.when(mine == place4)
        def _(place4=place4, pairs_of=pairs_of):
            products(place4, pairs_of, False, lhs, low, high, in_half)

    top_x[...] = jnp.broadcast_to(jnp.max(largest(xof, xsf)), top_x.shape)
    top_y[...] = jnp.broadcast_to(jnp.max(largest(yof, ysf)), top_y.shape)


def far_body(norm, low_in, high_in, top_x, top_y, xo, xop, xr, xrp, yo, yop, yr, yrp, *rest):
    own_ref, *send_refs = rest[:4]
    xof, xrf, yof, yrf, lhs, low, high = rest[4:]
    half, _, mine, line = place()
    in_half = xo.shape[1]
    for full, parts in ((xof, (xo, xop)), (xrf, (xr, xrp)), (yof, (yo, yop)), (yrf, (yr, yrp))):
        fill(full, parts, half, 0)
    low[...] = low_in[...]
    high[...] = high_in[...]
    for place4 in range(4):

        def pairs_of(a, even=place4 < 2):
            far_x, far_y = [(xrf, yof)], [(xof, yrf)]
            return (far_x if even else far_y, [], far_y if even else far_x)[a]

        @pl.when(mine == place4)
        def _(place4=place4, pairs_of=pairs_of):
            products(place4, pairs_of, True, lhs, low, high, in_half)

    bound_x = jnp.maximum(jnp.max(largest(xrf)), top_x[...])
    bound_y = jnp.maximum(jnp.max(largest(yrf)), top_y[...])
    bound = jnp.maximum(bound_x, 1e-14) * jnp.maximum(bound_y, 1e-14) * (2 * xo.shape[2] * norm)
    power = jnp.floor(jnp.log(TOP / bound) * (1.0 / math.log(2.0)))
    scale = jnp.exp2(power) * norm
    count = low.shape[1] // 2
    left = lax.broadcasted_iota(jnp.int32, (count, 128), 1) < 64
    for step in range(4):
        chunk = line ^ step
        even_low = low[chunk, pl.ds(0, count, stride=2), :]
        odd_low = pltpu.roll(low[chunk, pl.ds(1, count, stride=2), :], 64, 1)
        even_high = high[chunk, pl.ds(0, count, stride=2), :]
        odd_high = pltpu.roll(high[chunk, pl.ds(1, count, stride=2), :], 64, 1)
        by = norm if step == 0 else scale[0:1, :]
        out = own_ref if step == 0 else send_refs[step - 1]
        out[pl.ds(0, count, stride=3), :] = even_low * by
        out[pl.ds(1, count, stride=3), :] = jnp.where(left, even_high, odd_low) * by
        out[pl.ds(2, count, stride=3), :] = jnp.where(left, odd_low, odd_high) * by
        if step:
            out[3 * count : 3 * count + 2, :] = power[0:2, :]


def split_gradient(own, swap, relay, norm):
    (xo, xop, yo, yop), (xs, xsp, ys, ysp), (xr, xrp, yr, yrp) = own, swap, relay
    _, in_half, size = xo.shape
    out_half = yo.shape[1]
    rows = 27 * in_half // 8
    part = jax.ShapeDtypeStruct((4, rows, 128), F32)
    top = jax.ShapeDtypeStruct((8, 128), F32)
    full_x, full_y = pltpu.VMEM((2 * in_half, size), BF16), pltpu.VMEM((2 * out_half, size), BF16)
    lhs = pltpu.VMEM((1536, size), BF16)
    work = 4 * rows * 2 * out_half * 2 * size
    low, high, top_x, top_y = call(
        near_body,
        [part, part, top, top],
        [xo, xop, xs, xsp, yo, yop, ys, ysp],
        [full_x, full_x, full_y, full_y, lhs],
        4 * work // 3,
        "near",
    )
    flat = rows * 3 // 2
    outs = [jax.ShapeDtypeStruct((flat, 128), F32)] + [jax.ShapeDtypeStruct((flat + 2, 128), F32)] * 3
    total, *terms = call(
        functools.partial(far_body, norm),
        outs,
        [low, high, top_x, top_y, xo, xop, xr, xrp, yo, yop, yr, yrp],
        [full_x, full_x, full_y, full_y, lhs, pltpu.VMEM(part.shape, F32), pltpu.VMEM(part.shape, F32)],
        2 * work // 3,
        "far",
    )
    for step in (3, 2, 1):
        got = swapped(terms[step - 1].astype(jnp.float16), 4 * step).astype(F32)
        total = total + got[:flat] * jnp.exp2(-got[flat : flat + 1])
    return total.reshape(1, flat * 128)


def any_gradient(own, swap, relay, norm):
    count = lax.axis_size(AXIS)
    half, odd, _, _ = place()

    def whole(mine, other):
        parts = jnp.concatenate([mine, other], axis=1), jnp.concatenate([other, mine], axis=1)
        return jnp.where(half == 0, *parts)

    near, next_to, far = (whole(p[0], p[1]) for p in (own, swap, relay))
    cotangent = whole(own[2], own[3])[0]
    in_half, size = own[0].shape[1:]
    planes = [jnp.where(odd == 0, far, next_to), near, jnp.where(odd == 0, next_to, far)]
    column = jnp.arange(size, dtype=jnp.int32) % W
    found = []
    for plane in planes:
        mine = lax.dynamic_slice_in_dim(plane[0], half * in_half, in_half, 0)
        margin = jnp.pad(mine, [(0, 0), (W + 1, W + 1)])
        for b in range(3):
            for e in range(3):
                start = W * b + e
                here = (column + e - 1 >= 0) & (column + e - 1 < W)
                shifted = jnp.where(here, margin[:, start : start + size], jnp.zeros((), mine.dtype))
                found.append(jnp.einsum("kp,op->ko", shifted, cotangent, preferred_element_type=F32))
    term = jnp.stack(found).reshape(1, -1) * norm
    both = jnp.concatenate([jnp.where(half == 0, term, 0.0), jnp.where(half == 0, 0.0, term)])
    return lax.psum_scatter(both.reshape(count, -1), AXIS, scatter_dimension=0, tiled=True)


def local(activations, weights, cotangent):
    count = lax.axis_size(AXIS)
    size = activations.shape[2]
    next_x, next_y = swapped(activations, 2), swapped(cotangent, 2)
    other_x, other_y = swapped(activations, 1), swapped(cotangent, 1)
    far_x, far_y = relayed(next_x), relayed(next_y)
    next_other_x, next_other_y = swapped(next_x, 1), swapped(next_y, 1)
    far_other_x, far_other_y = swapped(far_x, 1), swapped(far_y, 1)
    own = (activations, other_x, cotangent, other_y)
    swap = (next_x, next_other_x, next_y, next_other_y)
    relay = (far_x, far_other_x, far_y, far_other_y)
    norm = 1.0 / math.sqrt(count // 2 * size)
    fits = count == 16 and activations.shape[1] == 96 and cotangent.shape[1] == 96
    gradient = (split_gradient if fits else any_gradient)(own, swap, relay, norm)
    tables = weight_tables(weights)
    xs = [part for plane in (own, swap, relay) for part in plane[:2]]
    ys = [part for plane in (own, swap, relay) for part in plane[2:]]
    forward, back = convolutions(xs, ys, tables)
    return forward, back, gradient


def solution(mesh):
    placed = P(("grp", AXIS), None, None)
    return jax.shard_map(
        local,
        mesh=mesh,
        in_specs=(placed, P(), placed),
        out_specs=(placed, placed, P(("grp", AXIS), None)),
        check_vma=False,
    )
```

```python
import functools
import math

import jax
import jax.numpy as jnp
from jax import lax
from jax.experimental import pallas as pl
from jax.experimental.pallas import tpu as pltpu
from jax.sharding import PartitionSpec as P

W = 64
AXIS = "slab"
F32 = jnp.float32
BF16 = jnp.bfloat16
TOP = 60000.0
IN_VMEM = pl.BlockSpec(memory_space=pltpu.VMEM)


def swapped(value, bit):
    count = lax.axis_size(AXIS)
    return lax.ppermute(value, AXIS, [(i, i ^ bit) for i in range(count)])


def relayed(value):
    count = lax.axis_size(AXIS)
    route = [(i, i - 4 if i & 2 else i + 4) for i in range(count)]
    return lax.ppermute(value, AXIS, [(i, j) for i, j in route if 0 <= j < count])


def place():
    index = lax.axis_index(AXIS)
    return index % 2, (index // 2) % 2, index % 4, index // 4


def call(body, outs, operands, scratch, flops, name):
    moved = sum(math.prod(a.shape) * a.dtype.itemsize for a in [*outs, *operands])
    return pl.pallas_call(
        body,
        out_shape=outs,
        in_specs=[IN_VMEM] * len(operands),
        out_specs=[IN_VMEM] * len(outs),
        scratch_shapes=scratch,
        cost_estimate=pl.CostEstimate(flops=flops, transcendentals=0, bytes_accessed=moved),
        compiler_params=pltpu.CompilerParams(vmem_limit_bytes=48 << 20),
        name=name,
    )(*operands)


def weight_body(w_ref, fwd_ref, back_ref):
    half, _, _, _ = place()
    chans, filters = w_ref.shape[3:]
    in_half, out_half = chans // 2, filters // 2
    start = pl.multiple_of(half * in_half, 32)
    for b in range(3):
        for e in range(3):
            block = 3 * b + e
            for a in range(3):
                turned = w_ref[a, b, e].T
                own = jnp.where(half == 0, turned[:out_half], turned[out_half:])
                fwd_ref[block * out_half : (block + 1) * out_half, a * chans : (a + 1) * chans] = own
                rows = w_ref[2 - a, 2 - b, 2 - e, pl.ds(start, in_half), :]
                back_ref[block * in_half : (block + 1) * in_half, a * filters : (a + 1) * filters] = rows


def weight_tables(weights):
    chans, filters = weights.shape[3:]
    outs = [
        jax.ShapeDtypeStruct((9 * filters // 2, 3 * chans), BF16),
        jax.ShapeDtypeStruct((9 * chans // 2, 3 * filters), BF16),
    ]
    return call(weight_body, outs, [weights], [], 0, "tables")


def fill(target, parts, half, first_row):
    rows = parts[0].shape[1]
    for part, which in zip(parts, (half, 1 - half)):
        target[pl.ds(pl.multiple_of(first_row + which * rows, 32), rows), :] = part[0]


def fold(product, out_ref, rows):
    size = product.shape[1]
    cell = lax.broadcasted_iota(jnp.int32, (rows, size), 1)
    column = cell % W

    def tap(b, e):
        block = 3 * b + e
        return product[block * rows : (block + 1) * rows, :]

    def over_rows(e):
        up = jnp.where(cell >= W, pltpu.roll(tap(0, e), W, 1), 0.0)
        down = jnp.where(cell < size - W, pltpu.roll(tap(2, e), size - W, 1), 0.0)
        return tap(1, e) + up + down

    left = jnp.where(column >= 1, pltpu.roll(over_rows(0), 1, 1), 0.0)
    right = jnp.where(column < W - 1, pltpu.roll(over_rows(2), size - 1, 1), 0.0)
    out_ref[0] = (over_rows(1) + left + right).astype(out_ref.dtype)


def conv_body(*refs):
    xs, ys = refs[0:6], refs[6:12]
    fwd_w, back_w, fwd_ref, back_ref, planes, product = refs[12:]
    half, odd, _, _ = place()
    for parts, table, out_ref in ((xs, fwd_w, fwd_ref), (ys, back_w, back_ref)):
        chans = 2 * parts[0].shape[1]
        for k, slot in enumerate((1, 2 - 2 * odd, 2 * odd)):
            fill(planes, parts[2 * k : 2 * k + 2], half, slot * chans)
        product[...] = jnp.dot(table[...], planes[...], preferred_element_type=F32)
        fold(product, out_ref, out_ref.shape[1])


def convolutions(xs, ys, tables):
    _, in_half, size = xs[0].shape
    out_half = ys[0].shape[1]
    outs = [
        jax.ShapeDtypeStruct((1, out_half, size), BF16),
        jax.ShapeDtypeStruct((1, in_half, size), BF16),
    ]
    scratch = [pltpu.VMEM((6 * in_half, size), BF16), pltpu.VMEM((9 * out_half, size), F32)]
    flops = 2 * 2 * 54 * in_half * out_half * size
    return call(conv_body, outs, [*xs, *ys, *tables], scratch, flops, "convolve")


def pieces(chunk, chunks, in_half):
    rows = 27 * in_half // chunks
    at, end, found = chunk * rows, (chunk + 1) * rows, []
    while at < end:
        tap, first = divmod(at, in_half)
        count = min(in_half - first, end - at)
        found.append((tap, first, count, at - chunk * rows))
        at += count
    return found


def moved(plane, b, e, cells):
    size = plane.shape[1]
    step = W * (b - 1) + e - 1
    if step:
        plane = pltpu.roll(plane, -step % size, 1)
    keep = None
    if b == 0:
        keep = cells >= W
    if b == 2:
        keep = cells < size - W
    if e != 1:
        inside = cells % W >= 1 if e == 0 else cells % W < W - 1
        keep = inside if keep is None else keep & inside
    return plane if keep is None else plane * keep.astype(F32).astype(plane.dtype)


def products(place4, pairs_of, accumulate, lhs, low, high, in_half):
    chunks = 8
    for a in range(3):
        pairs = pairs_of(a)
        rows = []
        for r in range(2):
            for tap, first, count, row in pieces(place4 + 4 * r, chunks, in_half):
                if tap // 9 == a:
                    begin, end = first // 16 * 16, -(-(first + count) // 16) * 16
                    rows.append((r, tap, first, count, row, begin, end))
        if not rows or not pairs:
            continue
        total = None
        for x_ref, y_ref in pairs:
            size = x_ref.shape[1]
            cells = lax.broadcasted_iota(jnp.int32, (1, size), 1)
            at = 0
            for r, tap, first, count, row, begin, end in rows:
                b, e = tap // 3 % 3, tap % 3
                for half in range(2):
                    source = x_ref[half * in_half + begin : half * in_half + end, :]
                    lhs[at : at + end - begin, :] = moved(source, b, e, cells)
                    at += end - begin
            term = lax.dot_general(
                lhs[0:at, :], y_ref[...], (((1,), (1,)), ((), ())), preferred_element_type=F32
            )
            total = term if total is None else total + term
        at = 0
        for r, tap, first, count, row, begin, end in rows:
            for half in range(2):
                got = total[at + first - begin : at + first - begin + count]
                at += end - begin
                chunk = 2 * half + r
                where = slice(row, row + count)
                if accumulate:
                    low[chunk, where, :] += got[:, :128]
                    high[chunk, where, 0:64] += got[:, 128:]
                else:
                    low[chunk, where, :] = got[:, :128]
                    high[chunk, where, 0:64] = got[:, 128:]


def largest(*refs):
    top = None
    for ref in refs:
        here = jnp.max(jnp.abs(ref[...].astype(F32)), axis=0, keepdims=True)
        top = here if top is None else jnp.maximum(top, here)
    return top


def near_body(xo, xop, xs, xsp, yo, yop, ys, ysp, low, high, top_x, top_y, xof, xsf, yof, ysf, lhs):
    half, _, mine, _ = place()
    in_half = xo.shape[1]
    for full, parts in ((xof, (xo, xop)), (xsf, (xs, xsp)), (yof, (yo, yop)), (ysf, (ys, ysp))):
        fill(full, parts, half, 0)
    high[...] = jnp.zeros_like(high)
    for place4 in range(4):
        lower, upper = ((xof, yof), (xsf, ysf)) if place4 < 2 else ((xsf, ysf), (xof, yof))

        def pairs_of(a, lower=lower, upper=upper):
            return ([(lower[0], upper[1])], [lower, upper], [(upper[0], lower[1])])[a]

        @pl.when(mine == place4)
        def _(place4=place4, pairs_of=pairs_of):
            products(place4, pairs_of, False, lhs, low, high, in_half)

    top_x[...] = jnp.broadcast_to(jnp.max(largest(xof, xsf)), top_x.shape)
    top_y[...] = jnp.broadcast_to(jnp.max(largest(yof, ysf)), top_y.shape)


def far_body(norm, low_in, high_in, top_x, top_y, xo, xop, xr, xrp, yo, yop, yr, yrp, *rest):
    own_ref, *send_refs = rest[:4]
    xof, xrf, yof, yrf, lhs, low, high = rest[4:]
    half, _, mine, line = place()
    in_half = xo.shape[1]
    for full, parts in ((xof, (xo, xop)), (xrf, (xr, xrp)), (yof, (yo, yop)), (yrf, (yr, yrp))):
        fill(full, parts, half, 0)
    low[...] = low_in[...]
    high[...] = high_in[...]
    for place4 in range(4):

        def pairs_of(a, even=place4 < 2):
            far_x, far_y = [(xrf, yof)], [(xof, yrf)]
            return (far_x if even else far_y, [], far_y if even else far_x)[a]

        @pl.when(mine == place4)
        def _(place4=place4, pairs_of=pairs_of):
            products(place4, pairs_of, True, lhs, low, high, in_half)

    bound_x = jnp.maximum(jnp.max(largest(xrf)), top_x[...])
    bound_y = jnp.maximum(jnp.max(largest(yrf)), top_y[...])
    bound = jnp.maximum(bound_x, 1e-14) * jnp.maximum(bound_y, 1e-14) * (2 * xo.shape[2] * norm)
    power = jnp.floor(jnp.log(TOP / bound) * (1.0 / math.log(2.0)))
    scale = jnp.exp2(power) * norm
    count = low.shape[1] // 2
    left = lax.broadcasted_iota(jnp.int32, (count, 128), 1) < 64
    for step in range(4):
        chunk = line ^ step
        even_low = low[chunk, pl.ds(0, count, stride=2), :]
        odd_low = pltpu.roll(low[chunk, pl.ds(1, count, stride=2), :], 64, 1)
        even_high = high[chunk, pl.ds(0, count, stride=2), :]
        odd_high = pltpu.roll(high[chunk, pl.ds(1, count, stride=2), :], 64, 1)
        by = norm if step == 0 else scale[0:1, :]
        out = own_ref if step == 0 else send_refs[step - 1]
        out[pl.ds(0, count, stride=3), :] = even_low * by
        out[pl.ds(1, count, stride=3), :] = jnp.where(left, even_high, odd_low) * by
        out[pl.ds(2, count, stride=3), :] = jnp.where(left, odd_low, odd_high) * by
        if step:
            out[3 * count : 3 * count + 2, :] = power[0:2, :]


def split_gradient(own, swap, relay, norm, near=None):
    (xo, xop, yo, yop), (xs, xsp, ys, ysp) = own, swap
    _, in_half, size = xo.shape
    out_half = yo.shape[1]
    rows = 27 * in_half // 8
    part = jax.ShapeDtypeStruct((4, rows, 128), F32)
    top = jax.ShapeDtypeStruct((8, 128), F32)
    full_x, full_y = pltpu.VMEM((2 * in_half, size), BF16), pltpu.VMEM((2 * out_half, size), BF16)
    lhs = pltpu.VMEM((1536, size), BF16)
    work = 4 * rows * 2 * out_half * 2 * size
    if near is None:
        return call(
            near_body,
            [part, part, top, top],
            [xo, xop, xs, xsp, yo, yop, ys, ysp],
            [full_x, full_x, full_y, full_y, lhs],
            4 * work // 3,
            "near",
        )
    low, high, top_x, top_y = near
    xr, xrp, yr, yrp = relay
    flat = rows * 3 // 2
    outs = [jax.ShapeDtypeStruct((flat, 128), F32)] + [jax.ShapeDtypeStruct((flat + 2, 128), F32)] * 3
    total, *terms = call(
        functools.partial(far_body, norm),
        outs,
        [low, high, top_x, top_y, xo, xop, xr, xrp, yo, yop, yr, yrp],
        [full_x, full_x, full_y, full_y, lhs, pltpu.VMEM(part.shape, F32), pltpu.VMEM(part.shape, F32)],
        2 * work // 3,
        "far",
    )
    for step in (3, 2, 1):
        got = swapped(terms[step - 1].astype(jnp.float16), 4 * step).astype(F32)
        total = total + got[:flat] * jnp.exp2(-got[flat : flat + 1])
    return total.reshape(1, flat * 128)


def any_gradient(own, swap, relay, norm):
    count = lax.axis_size(AXIS)
    half, odd, _, _ = place()

    def whole(mine, other):
        parts = jnp.concatenate([mine, other], axis=1), jnp.concatenate([other, mine], axis=1)
        return jnp.where(half == 0, *parts)

    near, next_to, far = (whole(p[0], p[1]) for p in (own, swap, relay))
    cotangent = whole(own[2], own[3])[0]
    in_half, size = own[0].shape[1:]
    planes = [jnp.where(odd == 0, far, next_to), near, jnp.where(odd == 0, next_to, far)]
    column = jnp.arange(size, dtype=jnp.int32) % W
    found = []
    for plane in planes:
        mine = lax.dynamic_slice_in_dim(plane[0], half * in_half, in_half, 0)
        margin = jnp.pad(mine, [(0, 0), (W + 1, W + 1)])
        for b in range(3):
            for e in range(3):
                start = W * b + e
                here = (column + e - 1 >= 0) & (column + e - 1 < W)
                shifted = jnp.where(here, margin[:, start : start + size], jnp.zeros((), mine.dtype))
                found.append(jnp.einsum("kp,op->ko", shifted, cotangent, preferred_element_type=F32))
    term = jnp.stack(found).reshape(1, -1) * norm
    both = jnp.concatenate([jnp.where(half == 0, term, 0.0), jnp.where(half == 0, 0.0, term)])
    return lax.psum_scatter(both.reshape(count, -1), AXIS, scatter_dimension=0, tiled=True)


def local(activations, weights, cotangent):
    count = lax.axis_size(AXIS)
    size = activations.shape[2]
    next_x, next_y = swapped(activations, 2), swapped(cotangent, 2)
    other_x, other_y = swapped(activations, 1), swapped(cotangent, 1)
    far_x, far_y = relayed(next_x), relayed(next_y)
    next_other_x, next_other_y = swapped(next_x, 1), swapped(next_y, 1)
    own = (activations, other_x, cotangent, other_y)
    swap = (next_x, next_other_x, next_y, next_other_y)
    norm = 1.0 / math.sqrt(count // 2 * size)
    fits = count == 16 and activations.shape[1] == 96 and cotangent.shape[1] == 96
    near = split_gradient(own, swap, None, norm) if fits else None
    tables = weight_tables(weights)
    far_x, far_y, near, tables = lax.optimization_barrier((far_x, far_y, near, tables))
    relay = (far_x, swapped(far_x, 1), far_y, swapped(far_y, 1))
    if fits:
        gradient = split_gradient(own, swap, relay, norm, near)
    else:
        gradient = any_gradient(own, swap, relay, norm)
    xs = [part for plane in (own, swap, relay) for part in plane[:2]]
    ys = [part for plane in (own, swap, relay) for part in plane[2:]]
    forward, back = convolutions(xs, ys, tables)
    return forward, back, gradient


def solution(mesh):
    placed = P(("grp", AXIS), None, None)
    return jax.shard_map(
        local,
        mesh=mesh,
        in_specs=(placed, P(), placed),
        out_specs=(placed, placed, P(("grp", AXIS), None)),
        check_vma=False,
    )
```

```python
import functools
import math

import jax
import jax.numpy as jnp
from jax import lax
from jax.experimental import pallas as pl
from jax.experimental.pallas import tpu as pltpu
from jax.sharding import PartitionSpec as P

W = 64
AXIS = "slab"
F32 = jnp.float32
BF16 = jnp.bfloat16
TOP = 60000.0
IN_VMEM = pl.BlockSpec(memory_space=pltpu.VMEM)


def swapped(value, bit):
    count = lax.axis_size(AXIS)
    return lax.ppermute(value, AXIS, [(i, i ^ bit) for i in range(count)])


def relayed(value):
    count = lax.axis_size(AXIS)
    up = [(i, i + 4 if i + 4 < count else i + 2) for i in range(count) if not i & 2]
    down = [(i, i - 4 if i >= 4 else i - 2) for i in range(count) if i & 2]
    return lax.ppermute(value, AXIS, up + down)


def handed(value):
    count = lax.axis_size(AXIS)
    route = [i ^ 1 if i in (0, 1, count - 2, count - 1) else i + 2 if i & 2 else i - 2 for i in range(count)]
    return lax.ppermute(value, AXIS, list(enumerate(route)))


def at_edge():
    index = lax.axis_index(AXIS) >> 1
    return (index == 0) | (index == lax.axis_size(AXIS) // 2 - 1)


def place():
    index = lax.axis_index(AXIS)
    return index & 1, (index >> 1) & 1, index & 3, index >> 2


def call(body, outs, operands, scratch, flops, name):
    moved = sum(math.prod(a.shape) * a.dtype.itemsize for a in [*outs, *operands])
    return pl.pallas_call(
        body,
        out_shape=outs,
        in_specs=[IN_VMEM] * len(operands),
        out_specs=[IN_VMEM] * len(outs),
        scratch_shapes=scratch,
        cost_estimate=pl.CostEstimate(flops=flops, transcendentals=0, bytes_accessed=moved),
        compiler_params=pltpu.CompilerParams(vmem_limit_bytes=20 << 20),
        name=name,
    )(*operands)


def stage_body(x_hbm, y_hbm, x_ref, y_ref, sems):
    copies = [
        pltpu.make_async_copy(source, target, sems.at[k])
        for k, (source, target) in enumerate(((x_hbm, x_ref), (y_hbm, y_ref)))
    ]
    for copy in copies:
        copy.start()
    for copy in copies:
        copy.wait()


def staged(*arrays):
    return pl.pallas_call(
        stage_body,
        out_shape=[pltpu.VMEM(a.shape, a.dtype) for a in arrays],
        in_specs=[pl.BlockSpec(memory_space=pltpu.HBM)] * len(arrays),
        out_specs=[IN_VMEM] * len(arrays),
        scratch_shapes=[pltpu.SemaphoreType.DMA((len(arrays),))],
        name="stage",
    )(*(pltpu.with_memory_space_constraint(a, pltpu.HBM) for a in arrays))


def weight_body(w_ref, fwd_ref, back_ref):
    half, _, _, _ = place()
    chans, filters = w_ref.shape[3:]
    in_half, out_half = chans // 2, filters // 2
    start = pl.multiple_of(half * in_half, 32)
    for b in range(3):
        for e in range(3):
            block = 3 * b + e
            for a in range(3):
                turned = w_ref[a, b, e].T
                own = jnp.where(half == 0, turned[:out_half], turned[out_half:])
                fwd_ref[block * out_half : (block + 1) * out_half, a * chans : (a + 1) * chans] = own
                rows = w_ref[2 - a, 2 - b, 2 - e, pl.ds(start, in_half), :]
                back_ref[block * in_half : (block + 1) * in_half, a * filters : (a + 1) * filters] = rows


def weight_tables(weights):
    chans, filters = weights.shape[3:]
    outs = [
        jax.ShapeDtypeStruct((9 * filters // 2, 3 * chans), BF16),
        jax.ShapeDtypeStruct((9 * chans // 2, 3 * filters), BF16),
    ]
    return call(weight_body, outs, [weights], [], 0, "tables")


def fill(target, parts, half, first_row, relay=False):
    rows = parts[0].shape[1]
    for part, which in zip(parts, (half, 1 - half)):
        value = part[0]
        if relay:
            value = jnp.where(at_edge(), jnp.zeros_like(value), value)
        target[pl.ds(pl.multiple_of(first_row + which * rows, 32), rows), :] = value


def fold(product, out_ref, rows):
    size = product.shape[1]
    cell = lax.broadcasted_iota(jnp.int32, (rows, size), 1)
    column = cell % W

    def tap(b, e):
        block = 3 * b + e
        return product[block * rows : (block + 1) * rows, :]

    def over_rows(e):
        up = jnp.where(cell >= W, pltpu.roll(tap(0, e), W, 1), 0.0)
        down = jnp.where(cell < size - W, pltpu.roll(tap(2, e), size - W, 1), 0.0)
        return tap(1, e) + up + down

    left = jnp.where(column >= 1, pltpu.roll(over_rows(0), 1, 1), 0.0)
    right = jnp.where(column < W - 1, pltpu.roll(over_rows(2), size - 1, 1), 0.0)
    out_ref[0] = (over_rows(1) + left + right).astype(out_ref.dtype)


def conv_body(*refs):
    xs, ys = refs[0:6], refs[6:12]
    fwd_w, back_w, fwd_ref, back_ref, planes, product = refs[12:]
    half, odd, _, _ = place()
    for parts, table, out_ref in ((xs, fwd_w, fwd_ref), (ys, back_w, back_ref)):
        chans = 2 * parts[0].shape[1]
        for k, slot in enumerate((1, 2 - 2 * odd, 2 * odd)):
            fill(planes, parts[2 * k : 2 * k + 2], half, slot * chans, relay=k == 2)
        product[...] = jnp.dot(table[...], planes[...], preferred_element_type=F32)
        fold(product, out_ref, out_ref.shape[1])


def convolutions(xs, ys, tables):
    _, in_half, size = xs[0].shape
    out_half = ys[0].shape[1]
    outs = [
        jax.ShapeDtypeStruct((1, out_half, size), BF16),
        jax.ShapeDtypeStruct((1, in_half, size), BF16),
    ]
    scratch = [pltpu.VMEM((6 * in_half, size), BF16), pltpu.VMEM((9 * out_half, size), F32)]
    flops = 2 * 2 * 54 * in_half * out_half * size
    return call(conv_body, outs, [*xs, *ys, *tables], scratch, flops, "convolve")


def pieces(chunk, chunks, in_half):
    rows = 27 * in_half // chunks
    at, end, found = chunk * rows, (chunk + 1) * rows, []
    while at < end:
        tap, first = divmod(at, in_half)
        count = min(in_half - first, end - at)
        found.append((tap, first, count, at - chunk * rows))
        at += count
    return found


def moved(plane, b, e, cells):
    size = plane.shape[1]
    step = W * (b - 1) + e - 1
    if step:
        plane = pltpu.roll(plane, -step % size, 1)
    keep = None
    if b == 0:
        keep = cells >= W
    if b == 2:
        keep = cells < size - W
    if e != 1:
        inside = cells % W >= 1 if e == 0 else cells % W < W - 1
        keep = inside if keep is None else keep & inside
    return plane if keep is None else plane * keep.astype(F32).astype(plane.dtype)


def products(place4, pairs_of, accumulate, lhs, low, high, in_half):
    chunks = 8
    for a in range(3):
        pairs = pairs_of(a)
        rows = []
        for r in range(2):
            for tap, first, count, row in pieces(place4 + 4 * r, chunks, in_half):
                if tap // 9 == a:
                    begin, end = first // 16 * 16, -(-(first + count) // 16) * 16
                    rows.append((r, tap, first, count, row, begin, end))
        if not rows or not pairs:
            continue
        total = None
        for x_ref, y_ref in pairs:
            size = x_ref.shape[1]
            cells = lax.broadcasted_iota(jnp.int32, (1, size), 1)
            at = 0
            for r, tap, first, count, row, begin, end in rows:
                b, e = tap // 3 % 3, tap % 3
                for half in range(2):
                    source = x_ref[half * in_half + begin : half * in_half + end, :]
                    lhs[at : at + end - begin, :] = moved(source, b, e, cells)
                    at += end - begin
            term = lax.dot_general(
                lhs[0:at, :], y_ref[...], (((1,), (1,)), ((), ())), preferred_element_type=F32
            )
            total = term if total is None else total + term
        at = 0
        for r, tap, first, count, row, begin, end in rows:
            for half in range(2):
                got = total[at + first - begin : at + first - begin + count]
                at += end - begin
                chunk = 2 * half + r
                where = slice(row, row + count)
                if accumulate:
                    low[chunk, where, :] += got[:, :128]
                    high[chunk, where, 0:64] += got[:, 128:]
                else:
                    low[chunk, where, :] = got[:, :128]
                    high[chunk, where, 0:64] = got[:, 128:]


def largest(*refs):
    top = None
    for ref in refs:
        here = jnp.max(jnp.abs(ref[...].astype(F32)), axis=0, keepdims=True)
        top = here if top is None else jnp.maximum(top, here)
    return top


def near_body(xo, xop, xs, xsp, yo, yop, ys, ysp, low, high, top_x, top_y, xof, xsf, yof, ysf, lhs):
    half, _, mine, _ = place()
    in_half = xo.shape[1]
    for full, parts in ((xof, (xo, xop)), (xsf, (xs, xsp)), (yof, (yo, yop)), (ysf, (ys, ysp))):
        fill(full, parts, half, 0)
    high[...] = jnp.zeros_like(high)
    for place4 in range(4):
        lower, upper = ((xof, yof), (xsf, ysf)) if place4 < 2 else ((xsf, ysf), (xof, yof))

        def pairs_of(a, lower=lower, upper=upper):
            return ([(lower[0], upper[1])], [lower, upper], [(upper[0], lower[1])])[a]

        @pl.when(mine == place4)
        def _(place4=place4, pairs_of=pairs_of):
            products(place4, pairs_of, False, lhs, low, high, in_half)

    top_x[...] = jnp.broadcast_to(jnp.max(largest(xof, xsf)), top_x.shape)
    top_y[...] = jnp.broadcast_to(jnp.max(largest(yof, ysf)), top_y.shape)


def far_body(norm, low_in, high_in, top_x, top_y, xo, xop, xr, xrp, yo, yop, yr, yrp, *rest):
    own_ref, *send_refs = rest[:4]
    xof, xrf, yof, yrf, lhs, low, high = rest[4:]
    half, _, mine, line = place()
    in_half = xo.shape[1]
    for full, parts in ((xof, (xo, xop)), (yof, (yo, yop))):
        fill(full, parts, half, 0)
    for full, parts in ((xrf, (xr, xrp)), (yrf, (yr, yrp))):
        fill(full, parts, half, 0, relay=True)
    low[...] = low_in[...]
    high[...] = high_in[...]
    for place4 in range(4):

        def pairs_of(a, even=place4 < 2):
            far_x, far_y = [(xrf, yof)], [(xof, yrf)]
            return (far_x if even else far_y, [], far_y if even else far_x)[a]

        @pl.when(mine == place4)
        def _(place4=place4, pairs_of=pairs_of):
            products(place4, pairs_of, True, lhs, low, high, in_half)

    bound_x = jnp.maximum(jnp.max(largest(xrf)), top_x[...])
    bound_y = jnp.maximum(jnp.max(largest(yrf)), top_y[...])
    bound = jnp.maximum(bound_x, 1e-14) * jnp.maximum(bound_y, 1e-14) * (2 * xo.shape[2] * norm)
    power = jnp.floor(jnp.log(TOP / bound) * (1.0 / math.log(2.0)))
    scale = jnp.exp2(power) * norm
    count = low.shape[1] // 2
    left = lax.broadcasted_iota(jnp.int32, (count, 128), 1) < 64
    for step in range(4):
        chunk = line ^ step
        even_low = low[chunk, pl.ds(0, count, stride=2), :]
        odd_low = pltpu.roll(low[chunk, pl.ds(1, count, stride=2), :], 64, 1)
        even_high = high[chunk, pl.ds(0, count, stride=2), :]
        odd_high = pltpu.roll(high[chunk, pl.ds(1, count, stride=2), :], 64, 1)
        by = norm if step == 0 else scale[0:1, :]
        out = own_ref if step == 0 else send_refs[step - 1]
        out[pl.ds(0, count, stride=3), :] = even_low * by
        out[pl.ds(1, count, stride=3), :] = jnp.where(left, even_high, odd_low) * by
        out[pl.ds(2, count, stride=3), :] = jnp.where(left, odd_low, odd_high) * by
        if step:
            out[3 * count : 3 * count + 2, :] = power[0:2, :]


def split_gradient(own, swap, relay, norm, later):
    (xo, xop, yo, yop), (xs, xsp, ys, ysp), (xr, xrp, yr, yrp) = own, swap, relay
    _, in_half, size = xo.shape
    out_half = yo.shape[1]
    rows = 27 * in_half // 8
    part = jax.ShapeDtypeStruct((4, rows, 128), F32)
    top = jax.ShapeDtypeStruct((8, 128), F32)
    full_x, full_y = pltpu.VMEM((2 * in_half, size), BF16), pltpu.VMEM((2 * out_half, size), BF16)
    lhs = pltpu.VMEM((1536, size), BF16)
    work = 4 * rows * 2 * out_half * 2 * size
    low, high, top_x, top_y = call(
        near_body,
        [part, part, top, top],
        [xo, xop, xs, xsp, yo, yop, ys, ysp],
        [full_x, full_x, full_y, full_y, lhs],
        4 * work // 3,
        "near",
    )
    flat = rows * 3 // 2
    outs = [jax.ShapeDtypeStruct((flat, 128), F32)] + [jax.ShapeDtypeStruct((flat + 2, 128), F32)] * 3
    total, *terms = call(
        functools.partial(far_body, norm),
        outs,
        [low, high, top_x, top_y, xo, xop, xr, xrp, yo, yop, yr, yrp],
        [full_x, full_x, full_y, full_y, lhs, pltpu.VMEM(part.shape, F32), pltpu.VMEM(part.shape, F32)],
        2 * work // 3,
        "far",
    )
    sent = [term.astype(jnp.float16) for term in terms]
    sent, later = lax.optimization_barrier((sent, later))
    gots = [swapped(sent[step - 1], 4 * step).astype(F32) for step in (2, 3, 1)]
    out = jax.ShapeDtypeStruct((flat, 1, 128), F32)
    return call(sum_body, [out], [total, *gots], [], 0, "sum")[0].reshape(1, flat * 128), later


def sum_body(own, *refs):
    gots, out_ref = refs[:-1], refs[-1]
    flat = own.shape[0]
    total = own[...]
    for got in gots:
        total = total + got[0:flat, :] * jnp.exp2(-got[flat : flat + 1, :])
    out_ref[:, 0, :] = total


def any_gradient(own, swap, relay, norm):
    count = lax.axis_size(AXIS)
    half, odd, _, _ = place()

    def whole(mine, other):
        parts = jnp.concatenate([mine, other], axis=1), jnp.concatenate([other, mine], axis=1)
        return jnp.where(half == 0, *parts)

    near, next_to, far = (whole(p[0], p[1]) for p in (own, swap, relay))
    cotangent = whole(own[2], own[3])[0]
    in_half, size = own[0].shape[1:]
    far = jnp.where(at_edge(), jnp.zeros_like(far), far)
    planes = [jnp.where(odd == 0, far, next_to), near, jnp.where(odd == 0, next_to, far)]
    column = jnp.arange(size, dtype=jnp.int32) % W
    found = []
    for plane in planes:
        mine = lax.dynamic_slice_in_dim(plane[0], half * in_half, in_half, 0)
        margin = jnp.pad(mine, [(0, 0), (W + 1, W + 1)])
        for b in range(3):
            for e in range(3):
                start = W * b + e
                here = (column + e - 1 >= 0) & (column + e - 1 < W)
                shifted = jnp.where(here, margin[:, start : start + size], jnp.zeros((), mine.dtype))
                found.append(jnp.einsum("kp,op->ko", shifted, cotangent, preferred_element_type=F32))
    term = jnp.stack(found).reshape(1, -1) * norm
    both = jnp.concatenate([jnp.where(half == 0, term, 0.0), jnp.where(half == 0, 0.0, term)])
    return lax.psum_scatter(both.reshape(count, -1), AXIS, scatter_dimension=0, tiled=True)


def local(activations, weights, cotangent):
    count = lax.axis_size(AXIS)
    size = activations.shape[2]
    next_x, next_y = swapped(activations, 2), swapped(cotangent, 2)
    own_x, own_y = staged(activations, cotangent)
    other_x, other_y = swapped(own_x, 1), swapped(own_y, 1)
    later_y, near_x = lax.optimization_barrier((cotangent, next_x))
    far_x, far_y = relayed(near_x), handed(later_y)
    next_other_x, next_other_y = swapped(next_x, 1), swapped(next_y, 1)
    far_other_x, far_other_y = swapped(far_x, 1), swapped(far_y, 1)
    own = (own_x, other_x, own_y, other_y)
    swap = (next_x, next_other_x, next_y, next_other_y)
    relay = (far_x, far_other_x, far_y, far_other_y)
    norm = 1.0 / math.sqrt(count // 2 * size)
    fits = count == 16 and activations.shape[1] == 96 and cotangent.shape[1] == 96
    if fits:
        gradient, weights = split_gradient(own, swap, relay, norm, weights)
    else:
        gradient = any_gradient(own, swap, relay, norm)
    tables = weight_tables(weights)
    xs = [part for plane in (own, swap, relay) for part in plane[:2]]
    ys = [part for plane in (own, swap, relay) for part in plane[2:]]
    forward, back = convolutions(xs, ys, tables)
    return forward, back, gradient


def solution(mesh):
    placed = P(("grp", AXIS), None, None)
    return jax.shard_map(
        local,
        mesh=mesh,
        in_specs=(placed, P(), placed),
        out_specs=(placed, placed, P(("grp", AXIS), None)),
        check_vma=False,
    )
```

```python
import functools
import math

import jax
import jax.numpy as jnp
from jax import lax
from jax.experimental import pallas as pl
from jax.experimental.pallas import tpu as pltpu
from jax.sharding import PartitionSpec as P

W = 64
AXIS = "slab"
F32 = jnp.float32
BF16 = jnp.bfloat16
TOP = 60000.0
CHUNKS = 8
IN_VMEM = pl.BlockSpec(memory_space=pltpu.VMEM)


def swapped(value, bit):
    count = lax.axis_size(AXIS)
    return lax.ppermute(value, AXIS, [(i, i ^ bit) for i in range(count)])


def relayed(value):
    count = lax.axis_size(AXIS)
    up = [(i, i + 4 if i + 4 < count else i + 2) for i in range(count) if not i & 2]
    down = [(i, i - 4 if i >= 4 else i - 2) for i in range(count) if i & 2]
    return lax.ppermute(value, AXIS, up + down)


def handed(value):
    count = lax.axis_size(AXIS)
    route = [i ^ 1 if i in (0, 1, count - 2, count - 1) else i + 2 if i & 2 else i - 2 for i in range(count)]
    return lax.ppermute(value, AXIS, list(enumerate(route)))


def at_edge():
    index = lax.axis_index(AXIS) >> 1
    return (index == 0) | (index == lax.axis_size(AXIS) // 2 - 1)


def place():
    index = lax.axis_index(AXIS)
    return index & 1, (index >> 1) & 1, index & 3, index >> 2


def call(body, outs, operands, scratch, flops, name):
    moved = sum(math.prod(a.shape) * a.dtype.itemsize for a in [*outs, *operands])
    return pl.pallas_call(
        body,
        out_shape=outs,
        in_specs=[IN_VMEM] * len(operands),
        out_specs=[IN_VMEM] * len(outs),
        scratch_shapes=scratch,
        cost_estimate=pl.CostEstimate(flops=flops, transcendentals=0, bytes_accessed=moved),
        compiler_params=pltpu.CompilerParams(vmem_limit_bytes=20 << 20),
        name=name,
    )(*operands)


def stage_body(x_hbm, y_hbm, x_ref, y_ref, sems):
    copies = [
        pltpu.make_async_copy(source, target, sems.at[k])
        for k, (source, target) in enumerate(((x_hbm, x_ref), (y_hbm, y_ref)))
    ]
    for copy in copies:
        copy.start()
    for copy in copies:
        copy.wait()


def staged(*arrays):
    return pl.pallas_call(
        stage_body,
        out_shape=[pltpu.VMEM(a.shape, a.dtype) for a in arrays],
        in_specs=[pl.BlockSpec(memory_space=pltpu.HBM)] * len(arrays),
        out_specs=[IN_VMEM] * len(arrays),
        scratch_shapes=[pltpu.SemaphoreType.DMA((len(arrays),))],
        name="stage",
    )(*(pltpu.with_memory_space_constraint(a, pltpu.HBM) for a in arrays))


def weight_body(w_ref, fwd_ref, back_ref):
    half, _, _, _ = place()
    chans, filters = w_ref.shape[3:]
    in_half, out_half = chans // 2, filters // 2
    start = pl.multiple_of(half * in_half, 32)
    for b in range(3):
        for e in range(3):
            block = 3 * b + e
            for a in range(3):
                turned = w_ref[a, b, e].T
                own = jnp.where(half == 0, turned[:out_half], turned[out_half:])
                fwd_ref[block * out_half : (block + 1) * out_half, a * chans : (a + 1) * chans] = own
                rows = w_ref[2 - a, 2 - b, 2 - e, pl.ds(start, in_half), :]
                back_ref[block * in_half : (block + 1) * in_half, a * filters : (a + 1) * filters] = rows


def weight_tables(weights):
    chans, filters = weights.shape[3:]
    outs = [
        jax.ShapeDtypeStruct((9 * filters // 2, 3 * chans), BF16),
        jax.ShapeDtypeStruct((9 * chans // 2, 3 * filters), BF16),
    ]
    return call(weight_body, outs, [weights], [], 0, "tables")


def fill(target, parts, half, first_row, relay=False):
    rows = parts[0].shape[1]
    for part, which in zip(parts, (half, 1 - half)):
        value = part[0]
        if relay:
            value = jnp.where(at_edge(), jnp.zeros_like(value), value)
        target[pl.ds(pl.multiple_of(first_row + which * rows, 32), rows), :] = value


def fold(product, out_ref, rows):
    size = product.shape[1]
    cell = lax.broadcasted_iota(jnp.int32, (rows, size), 1)
    column = cell % W

    def tap(b, e):
        block = 3 * b + e
        return product[block * rows : (block + 1) * rows, :]

    def over_rows(e):
        up = jnp.where(cell >= W, pltpu.roll(tap(0, e), W, 1), 0.0)
        down = jnp.where(cell < size - W, pltpu.roll(tap(2, e), size - W, 1), 0.0)
        return tap(1, e) + up + down

    left = jnp.where(column >= 1, pltpu.roll(over_rows(0), 1, 1), 0.0)
    right = jnp.where(column < W - 1, pltpu.roll(over_rows(2), size - 1, 1), 0.0)
    out_ref[0] = (over_rows(1) + left + right).astype(out_ref.dtype)


def conv_body(*refs):
    xs, ys = refs[0:6], refs[6:12]
    fwd_w, back_w, fwd_ref, back_ref, planes, product = refs[12:]
    half, odd, _, _ = place()
    for parts, table, out_ref in ((xs, fwd_w, fwd_ref), (ys, back_w, back_ref)):
        chans = 2 * parts[0].shape[1]
        for k, slot in enumerate((1, 2 - 2 * odd, 2 * odd)):
            fill(planes, parts[2 * k : 2 * k + 2], half, slot * chans, relay=k == 2)
        product[...] = jnp.dot(table[...], planes[...], preferred_element_type=F32)
        fold(product, out_ref, out_ref.shape[1])


def convolutions(xs, ys, tables):
    _, in_half, size = xs[0].shape
    out_half = ys[0].shape[1]
    outs = [
        jax.ShapeDtypeStruct((1, out_half, size), BF16),
        jax.ShapeDtypeStruct((1, in_half, size), BF16),
    ]
    scratch = [pltpu.VMEM((6 * in_half, size), BF16), pltpu.VMEM((9 * out_half, size), F32)]
    flops = 2 * 2 * 54 * in_half * out_half * size
    return call(conv_body, outs, [*xs, *ys, *tables], scratch, flops, "convolve")


def pieces(chunk, chunks, in_half):
    rows = 27 * in_half // chunks
    at, end, found = chunk * rows, (chunk + 1) * rows, []
    while at < end:
        tap, first = divmod(at, in_half)
        count = min(in_half - first, end - at)
        found.append((tap, first, count, at - chunk * rows))
        at += count
    return found


def moved(plane, b, e, cells):
    size = plane.shape[1]
    step = W * (b - 1) + e - 1
    if step:
        plane = pltpu.roll(plane, -step % size, 1)
    keep = None
    if b == 0:
        keep = cells >= W
    if b == 2:
        keep = cells < size - W
    if e != 1:
        inside = cells % W >= 1 if e == 0 else cells % W < W - 1
        keep = inside if keep is None else keep & inside
    return plane if keep is None else plane * keep.astype(F32).astype(plane.dtype)


def products(place4, r, pairs_of, accumulate, halves, lhs, low, high, in_half):
    for a in range(3):
        pairs = pairs_of(a)
        rows = []
        for tap, first, count, row in pieces(place4 + 4 * r, CHUNKS, in_half):
            if tap // 9 == a:
                begin, end = first // 16 * 16, -(-(first + count) // 16) * 16
                rows += [(k, tap, first, count, row, begin, end) for k in range(len(halves))]
        if not rows or not pairs:
            continue
        total = None
        for x_ref, y_ref in pairs:
            size = x_ref.shape[1]
            cells = lax.broadcasted_iota(jnp.int32, (1, size), 1)
            at = 0
            for k, tap, first, count, row, begin, end in rows:
                start = pl.multiple_of(halves[k] * in_half + begin, 16)
                source = x_ref[pl.ds(start, end - begin), :]
                lhs[at : at + end - begin, :] = moved(source, tap // 3 % 3, tap % 3, cells)
                at += end - begin
            term = lax.dot_general(
                lhs[0:at, :], y_ref[...], (((1,), (1,)), ((), ())), preferred_element_type=F32
            )
            total = term if total is None else total + term
        at = 0
        for k, tap, first, count, row, begin, end in rows:
            got = total[at + first - begin : at + first - begin + count]
            at += end - begin
            where = slice(row, row + count)
            if accumulate:
                low[k, where, :] += got[:, :128]
                high[k, where, 0:64] += got[:, 128:]
            else:
                low[k, where, :] = got[:, :128]
                high[k, where, 0:64] = got[:, 128:]


def at_place(run):
    _, _, mine, line = place()
    for place4 in range(4):
        for r in range(2):
            pl.when((mine == place4) & ((line & 1) == r))(functools.partial(run, place4, r))


def pairs_for(own, swap, far, even):
    (xo, yo), (xs, ys), (xf, yf) = own, swap, far
    lower, upper = ((xo, yo), (xs, ys)) if even else ((xs, ys), (xo, yo))
    near = ([(lower[0], upper[1])], [lower, upper], [(upper[0], lower[1])])
    first, last = [(xf, yo)], [(xo, yf)]
    return near, (first if even else last, [], last if even else first)


def gather_planes(parts, fulls, half):
    for k, (xa, xb, ya, yb) in enumerate(parts):
        fill(fulls[2 * k], (xa, xb), half, 0, relay=k == 2)
        fill(fulls[2 * k + 1], (ya, yb), half, 0, relay=k == 2)


def near_body(*refs):
    parts, (low, high), fulls, lhs = (refs[0:4], refs[4:8]), refs[8:10], refs[10:14], refs[14]
    half, _, _, line = place()
    gather_planes(parts, fulls, half)
    high[...] = jnp.zeros_like(high)

    def run(place4, r):
        near, _ = pairs_for(fulls[0:2], fulls[2:4], (None, None), place4 < 2)
        products(
            place4, r, lambda a: near[a], False, [(line >> 1) ^ 1], lhs, low, high, parts[0][0].shape[1]
        )

    at_place(run)


def emit(low, high, row, norm, out, plain=False):
    count = low.shape[1] // 2
    if plain:
        by = norm
    else:
        top = jnp.maximum(jnp.max(jnp.abs(low[row])), jnp.max(jnp.abs(high[row])))
        top = jnp.maximum(jnp.broadcast_to(top, (8, 128)) * norm, 1e-25)
        power = jnp.floor(jnp.log(TOP / top) * (1.0 / math.log(2.0)))
        out[3 * count : 3 * count + 2, :] = power[0:2]
        by = jnp.exp2(power)[0:1] * norm
    left = lax.broadcasted_iota(jnp.int32, (count, 128), 1) < 64
    even_low = low[row, pl.ds(0, count, stride=2), :]
    odd_low = pltpu.roll(low[row, pl.ds(1, count, stride=2), :], 64, 1)
    even_high = high[row, pl.ds(0, count, stride=2), :]
    odd_high = pltpu.roll(high[row, pl.ds(1, count, stride=2), :], 64, 1)
    out[pl.ds(0, count, stride=3), :] = even_low * by
    out[pl.ds(1, count, stride=3), :] = jnp.where(left, even_high, odd_low) * by
    out[pl.ds(2, count, stride=3), :] = jnp.where(left, odd_low, odd_high) * by


def far_body(norm, low_in, high_in, *refs):
    parts, out_ref, rest = (refs[0:4], refs[4:8]), refs[8], refs[9:]
    fulls, lhs, low, high = rest[0:4], rest[4], rest[5], rest[6]
    half, _, _, line = place()
    fill(fulls[0], parts[0][0:2], half, 0)
    fill(fulls[1], parts[0][2:4], half, 0)
    fill(fulls[2], parts[1][0:2], half, 0, relay=True)
    fill(fulls[3], parts[1][2:4], half, 0, relay=True)
    low[...] = low_in[...]
    high[...] = high_in[...]

    def run(place4, r):
        _, far = pairs_for(fulls[0:2], (None, None), fulls[2:4], place4 < 2)
        products(
            place4, r, lambda a: far[a], True, [(line >> 1) ^ 1], lhs, low, high, parts[0][0].shape[1]
        )

    at_place(run)
    emit(low, high, 0, norm, out_ref)


def rest_body(own, norm, *refs):
    parts, outs = (refs[0:4], refs[4:8], refs[8:12]), refs[12 : 13 if own else 14]
    rest = refs[12 + len(outs) :]
    fulls, lhs, low, high = rest[0:6], rest[6], rest[7], rest[8]
    half, _, _, line = place()
    gather_planes(parts, fulls, half)
    high[...] = jnp.zeros_like(high)
    halves = [line >> 1] if own else [line >> 1, (line >> 1) ^ 1]

    def run(place4, r):
        near, far = pairs_for(fulls[0:2], fulls[2:4], fulls[4:6], place4 < 2)
        chosen = r if own else 1 - r
        products(
            place4, chosen, lambda a: near[a] + far[a], False, halves, lhs, low, high, parts[0][0].shape[1]
        )

    at_place(run)
    for k, out in enumerate(outs):
        emit(low, high, k, norm, out, plain=own)


def split_gradient(own, swap, relay, norm):
    own, swap, relay = ((x, xp, y, yp) for x, xp, y, yp in (own, swap, relay))
    _, in_half, size = own[0].shape
    out_half = own[2].shape[1]
    rows = 27 * in_half // CHUNKS
    flat = rows * 3 // 2
    part = jax.ShapeDtypeStruct((1, rows, 128), F32)
    sent = jax.ShapeDtypeStruct((flat + 2, 128), F32)
    mine = jax.ShapeDtypeStruct((flat, 128), F32)
    planes = [pltpu.VMEM((2 * in_half, size), BF16), pltpu.VMEM((2 * out_half, size), BF16)]
    lhs = pltpu.VMEM((1024, size), BF16)
    work = rows * 2 * out_half * 2 * size

    def sums(chunks):
        return [pltpu.VMEM((chunks, rows, 128), F32)] * 2

    near = call(near_body, [part, part], [*own, *swap], [*planes * 2, lhs], 4 * work // 3, "near")
    term = call(
        functools.partial(far_body, norm),
        [sent],
        [*near, *own, *relay],
        [*planes * 2, lhs, *sums(1)],
        2 * work // 3,
        "far",
    )[0].astype(jnp.float16)
    term, first = lax.optimization_barrier((term, own[0]))
    gots = [swapped(term, 8)]

    def rest(mine_too, shapes, x):
        body = functools.partial(rest_body, mine_too, norm)
        scratch = [*planes * 3, lhs, *sums(len(shapes))]
        return call(body, shapes, [x, *own[1:], *swap, *relay], scratch, 2 * work * len(shapes), "rest")

    sides = [side.astype(jnp.float16) for side in rest(False, [sent, sent], first)]
    sides, first = lax.optimization_barrier((sides, first))
    gots += [swapped(sides[0], 4), swapped(sides[1], 12)]
    (kept,) = rest(True, [mine], first)
    out = jax.ShapeDtypeStruct((flat, 1, 128), F32)
    operands = [kept, *(got.astype(F32) for got in gots)]
    return call(sum_body, [out], operands, [], 0, "sum")[0].reshape(1, flat * 128)


def sum_body(own, *refs):
    gots, out_ref = refs[:-1], refs[-1]
    flat = own.shape[0]
    total = own[...]
    for got in gots:
        total = total + got[0:flat, :] * jnp.exp2(-got[flat : flat + 1, :])
    out_ref[:, 0, :] = total


def any_gradient(own, swap, relay, norm):
    count = lax.axis_size(AXIS)
    half, odd, _, _ = place()

    def whole(mine, other):
        parts = jnp.concatenate([mine, other], axis=1), jnp.concatenate([other, mine], axis=1)
        return jnp.where(half == 0, *parts)

    near, next_to, far = (whole(p[0], p[1]) for p in (own, swap, relay))
    cotangent = whole(own[2], own[3])[0]
    in_half, size = own[0].shape[1:]
    far = jnp.where(at_edge(), jnp.zeros_like(far), far)
    planes = [jnp.where(odd == 0, far, next_to), near, jnp.where(odd == 0, next_to, far)]
    column = jnp.arange(size, dtype=jnp.int32) % W
    found = []
    for plane in planes:
        mine = lax.dynamic_slice_in_dim(plane[0], half * in_half, in_half, 0)
        margin = jnp.pad(mine, [(0, 0), (W + 1, W + 1)])
        for b in range(3):
            for e in range(3):
                start = W * b + e
                here = (column + e - 1 >= 0) & (column + e - 1 < W)
                shifted = jnp.where(here, margin[:, start : start + size], jnp.zeros((), mine.dtype))
                found.append(jnp.einsum("kp,op->ko", shifted, cotangent, preferred_element_type=F32))
    term = jnp.stack(found).reshape(1, -1) * norm
    both = jnp.concatenate([jnp.where(half == 0, term, 0.0), jnp.where(half == 0, 0.0, term)])
    return lax.psum_scatter(both.reshape(count, -1), AXIS, scatter_dimension=0, tiled=True)


def local(activations, weights, cotangent):
    count = lax.axis_size(AXIS)
    size = activations.shape[2]
    next_x = swapped(activations, 2)
    own_x, own_y = staged(activations, cotangent)
    next_y = swapped(own_y, 2)
    later_y, near_x = lax.optimization_barrier((own_y, next_x))
    far_x, far_y = relayed(near_x), handed(later_y)
    other_x, other_y = swapped(own_x, 1), swapped(own_y, 1)
    tables = weight_tables(weights)
    later_x, tables = lax.optimization_barrier((next_x, tables))
    next_other_x, next_other_y = swapped(later_x, 1), swapped(next_y, 1)
    far_other_x, far_other_y = swapped(far_x, 1), swapped(far_y, 1)
    own = (own_x, other_x, own_y, other_y)
    swap = (next_x, next_other_x, next_y, next_other_y)
    relay = (far_x, far_other_x, far_y, far_other_y)
    norm = 1.0 / math.sqrt(count // 2 * size)
    fits = count == 16 and activations.shape[1] == 96 and cotangent.shape[1] == 96
    if fits:
        gradient = split_gradient(own, swap, relay, norm)
    else:
        gradient = any_gradient(own, swap, relay, norm)
    xs = [part for plane in (own, swap, relay) for part in plane[:2]]
    ys = [part for plane in (own, swap, relay) for part in plane[2:]]
    forward, back = convolutions(xs, ys, tables)
    return forward, back, gradient


def solution(mesh):
    placed = P(("grp", AXIS), None, None)
    return jax.shard_map(
        local,
        mesh=mesh,
        in_specs=(placed, P(), placed),
        out_specs=(placed, placed, P(("grp", AXIS), None)),
        check_vma=False,
    )
```

```python
import functools
import math

import jax
import jax.numpy as jnp
from jax import lax
from jax.experimental import pallas as pl
from jax.experimental.pallas import tpu as pltpu
from jax.sharding import PartitionSpec as P

W = 64
AXIS = "slab"
F32 = jnp.float32
BF16 = jnp.bfloat16
TOP = 60000.0
CHUNKS = 8
IN_VMEM = pl.BlockSpec(memory_space=pltpu.VMEM)


def swapped(value, bit):
    count = lax.axis_size(AXIS)
    return lax.ppermute(value, AXIS, [(i, i ^ bit) for i in range(count)])


def relayed(value):
    count = lax.axis_size(AXIS)
    up = [(i, i + 4 if i + 4 < count else i + 2) for i in range(count) if not i & 2]
    down = [(i, i - 4 if i >= 4 else i - 2) for i in range(count) if i & 2]
    return lax.ppermute(value, AXIS, up + down)


def handed(value):
    count = lax.axis_size(AXIS)
    route = [i ^ 1 if i in (0, 1, count - 2, count - 1) else i + 2 if i & 2 else i - 2 for i in range(count)]
    return lax.ppermute(value, AXIS, list(enumerate(route)))


def at_edge():
    index = lax.axis_index(AXIS) >> 1
    return (index == 0) | (index == lax.axis_size(AXIS) // 2 - 1)


def place():
    index = lax.axis_index(AXIS)
    return index & 1, (index >> 1) & 1, index & 3, index >> 2


def call(body, outs, operands, scratch, flops, name):
    moved = sum(math.prod(a.shape) * a.dtype.itemsize for a in [*outs, *operands])
    return pl.pallas_call(
        body,
        out_shape=outs,
        in_specs=[IN_VMEM] * len(operands),
        out_specs=[IN_VMEM] * len(outs),
        scratch_shapes=scratch,
        cost_estimate=pl.CostEstimate(flops=flops, transcendentals=0, bytes_accessed=moved),
        compiler_params=pltpu.CompilerParams(vmem_limit_bytes=20 << 20),
        name=name,
    )(*operands)


def stage_body(x_hbm, y_hbm, x_ref, y_ref, sems):
    copies = [
        pltpu.make_async_copy(source, target, sems.at[k])
        for k, (source, target) in enumerate(((x_hbm, x_ref), (y_hbm, y_ref)))
    ]
    for copy in copies:
        copy.start()
    for copy in copies:
        copy.wait()


def staged(*arrays):
    return pl.pallas_call(
        stage_body,
        out_shape=[pltpu.VMEM(a.shape, a.dtype) for a in arrays],
        in_specs=[pl.BlockSpec(memory_space=pltpu.HBM)] * len(arrays),
        out_specs=[IN_VMEM] * len(arrays),
        scratch_shapes=[pltpu.SemaphoreType.DMA((len(arrays),))],
        name="stage",
    )(*(pltpu.with_memory_space_constraint(a, pltpu.HBM) for a in arrays))


def weight_body(w_ref, fwd_ref, back_ref):
    half, _, _, _ = place()
    chans, filters = w_ref.shape[3:]
    in_half, out_half = chans // 2, filters // 2
    start = pl.multiple_of(half * in_half, 32)
    for b in range(3):
        for e in range(3):
            block = 3 * b + e
            for a in range(3):
                turned = w_ref[a, b, e].T
                own = jnp.where(half == 0, turned[:out_half], turned[out_half:])
                fwd_ref[block * out_half : (block + 1) * out_half, a * chans : (a + 1) * chans] = own
                rows = w_ref[2 - a, 2 - b, 2 - e, pl.ds(start, in_half), :]
                back_ref[block * in_half : (block + 1) * in_half, a * filters : (a + 1) * filters] = rows


def weight_tables(weights):
    chans, filters = weights.shape[3:]
    outs = [
        jax.ShapeDtypeStruct((9 * filters // 2, 3 * chans), BF16),
        jax.ShapeDtypeStruct((9 * chans // 2, 3 * filters), BF16),
    ]
    return call(weight_body, outs, [weights], [], 0, "tables")


def fill(target, parts, half, first_row, relay=False):
    rows = parts[0].shape[1]
    for part, which in zip(parts, (half, 1 - half)):
        value = part[0]
        if relay:
            value = jnp.where(at_edge(), jnp.zeros_like(value), value)
        target[pl.ds(pl.multiple_of(first_row + which * rows, 32), rows), :] = value


def fold(product, out_ref, rows):
    size = product.shape[1]
    cell = lax.broadcasted_iota(jnp.int32, (rows, size), 1)
    column = cell % W

    def tap(b, e):
        block = 3 * b + e
        return product[block * rows : (block + 1) * rows, :]

    def over_rows(e):
        up = jnp.where(cell >= W, pltpu.roll(tap(0, e), W, 1), 0.0)
        down = jnp.where(cell < size - W, pltpu.roll(tap(2, e), size - W, 1), 0.0)
        return tap(1, e) + up + down

    left = jnp.where(column >= 1, pltpu.roll(over_rows(0), 1, 1), 0.0)
    right = jnp.where(column < W - 1, pltpu.roll(over_rows(2), size - 1, 1), 0.0)
    out_ref[0] = (over_rows(1) + left + right).astype(out_ref.dtype)


def conv_body(*refs):
    xs, ys = refs[0:6], refs[6:12]
    fwd_w, back_w, fwd_ref, back_ref, planes, product = refs[12:]
    half, odd, _, _ = place()
    for parts, table, out_ref in ((xs, fwd_w, fwd_ref), (ys, back_w, back_ref)):
        chans = 2 * parts[0].shape[1]
        for k, slot in enumerate((1, 2 - 2 * odd, 2 * odd)):
            fill(planes, parts[2 * k : 2 * k + 2], half, slot * chans, relay=k == 2)
        product[...] = jnp.dot(table[...], planes[...], preferred_element_type=F32)
        fold(product, out_ref, out_ref.shape[1])


def convolutions(xs, ys, tables):
    _, in_half, size = xs[0].shape
    out_half = ys[0].shape[1]
    outs = [
        jax.ShapeDtypeStruct((1, out_half, size), BF16),
        jax.ShapeDtypeStruct((1, in_half, size), BF16),
    ]
    scratch = [pltpu.VMEM((6 * in_half, size), BF16), pltpu.VMEM((9 * out_half, size), F32)]
    flops = 2 * 2 * 54 * in_half * out_half * size
    return call(conv_body, outs, [*xs, *ys, *tables], scratch, flops, "convolve")


def pieces(chunk, chunks, in_half):
    rows = 27 * in_half // chunks
    at, end, found = chunk * rows, (chunk + 1) * rows, []
    while at < end:
        tap, first = divmod(at, in_half)
        count = min(in_half - first, end - at)
        found.append((tap, first, count, at - chunk * rows))
        at += count
    return found


def moved(plane, b, e, cells):
    size = plane.shape[1]
    step = W * (b - 1) + e - 1
    if step:
        plane = pltpu.roll(plane, -step % size, 1)
    keep = None
    if b == 0:
        keep = cells >= W
    if b == 2:
        keep = cells < size - W
    if e != 1:
        inside = cells % W >= 1 if e == 0 else cells % W < W - 1
        keep = inside if keep is None else keep & inside
    return plane if keep is None else plane * keep.astype(F32).astype(plane.dtype)


def products(place4, r, pairs_of, accumulate, halves, lhs, low, high, in_half):
    for a in range(3):
        pairs = pairs_of(a)
        rows = []
        for tap, first, count, row in pieces(place4 + 4 * r, CHUNKS, in_half):
            if tap // 9 == a:
                begin, end = first // 16 * 16, -(-(first + count) // 16) * 16
                rows += [(k, tap, first, count, row, begin, end) for k in range(len(halves))]
        if not rows or not pairs:
            continue
        total = None
        for x_ref, y_ref in pairs:
            size = x_ref.shape[1]
            cells = lax.broadcasted_iota(jnp.int32, (1, size), 1)
            at = 0
            for k, tap, first, count, row, begin, end in rows:
                start = pl.multiple_of(halves[k] * in_half + begin, 16)
                source = x_ref[pl.ds(start, end - begin), :]
                lhs[at : at + end - begin, :] = moved(source, tap // 3 % 3, tap % 3, cells)
                at += end - begin
            term = lax.dot_general(
                lhs[0:at, :], y_ref[...], (((1,), (1,)), ((), ())), preferred_element_type=F32
            )
            total = term if total is None else total + term
        at = 0
        for k, tap, first, count, row, begin, end in rows:
            got = total[at + first - begin : at + first - begin + count]
            at += end - begin
            where = slice(row, row + count)
            if accumulate:
                low[k, where, :] += got[:, :128]
                high[k, where, 0:64] += got[:, 128:]
            else:
                low[k, where, :] = got[:, :128]
                high[k, where, 0:64] = got[:, 128:]


def at_place(run):
    _, _, mine, line = place()
    for place4 in range(4):
        for r in range(2):
            pl.when((mine == place4) & ((line & 1) == r))(functools.partial(run, place4, r))


def pairs_for(own, swap, far, even):
    (xo, yo), (xs, ys), (xf, yf) = own, swap, far
    lower, upper = ((xo, yo), (xs, ys)) if even else ((xs, ys), (xo, yo))
    near = ([(lower[0], upper[1])], [lower, upper], [(upper[0], lower[1])])
    first, last = [(xf, yo)], [(xo, yf)]
    return near, (first if even else last, [], last if even else first)


def near_body(xo, xop, yo, yop, xs, xsp, ys, ysp, low, high, *rest):
    fulls, lhs = rest[0:4], rest[4]
    half, _, _, line = place()
    for full, parts in zip(fulls, ((xo, xop), (yo, yop), (xs, xsp), (ys, ysp))):
        fill(full, parts, half, 0)
    high[...] = jnp.zeros_like(high)

    def run(place4, r):
        near, _ = pairs_for(fulls[0:2], fulls[2:4], (None, None), place4 < 2)
        products(place4, r, lambda a: near[a], False, [(line >> 1) ^ 1], lhs, low, high, xo.shape[1])

    at_place(run)


def emit(low, high, row, norm, out, plain=False):
    count = low.shape[1] // 2
    if plain:
        by = norm
    else:
        top = jnp.maximum(jnp.max(jnp.abs(low[row])), jnp.max(jnp.abs(high[row])))
        top = jnp.maximum(jnp.broadcast_to(top, (8, 128)) * norm, 1e-25)
        power = jnp.floor(jnp.log(TOP / top) * (1.0 / math.log(2.0)))
        out[3 * count : 3 * count + 2, :] = power[0:2]
        by = jnp.exp2(power)[0:1] * norm
    left = lax.broadcasted_iota(jnp.int32, (count, 128), 1) < 64
    even_low = low[row, pl.ds(0, count, stride=2), :]
    odd_low = pltpu.roll(low[row, pl.ds(1, count, stride=2), :], 64, 1)
    even_high = high[row, pl.ds(0, count, stride=2), :]
    odd_high = pltpu.roll(high[row, pl.ds(1, count, stride=2), :], 64, 1)
    out[pl.ds(0, count, stride=3), :] = even_low * by
    out[pl.ds(1, count, stride=3), :] = jnp.where(left, even_high, odd_low) * by
    out[pl.ds(2, count, stride=3), :] = jnp.where(left, odd_low, odd_high) * by


def far_body(norm, low_in, high_in, xof, yof, xr, xrp, yr, yrp, out_ref, xrf, yrf, lhs, low, high):
    half, _, _, line = place()
    fill(xrf, (xr, xrp), half, 0, relay=True)
    fill(yrf, (yr, yrp), half, 0, relay=True)
    low[...] = low_in[...]
    high[...] = high_in[...]

    def run(place4, r):
        _, far = pairs_for((xof, yof), (None, None), (xrf, yrf), place4 < 2)
        products(place4, r, lambda a: far[a], True, [(line >> 1) ^ 1], lhs, low, high, xr.shape[1])

    at_place(run)
    emit(low, high, 0, norm, out_ref)


def rest_body(step, norm, *refs):
    fulls, (out_ref, lhs, low, high) = refs[0:6], refs[6:]
    _, _, _, line = place()
    in_half = fulls[0].shape[0] // 2
    high[...] = jnp.zeros_like(high)

    def run(place4, r):
        near, far = pairs_for(fulls[0:2], fulls[2:4], fulls[4:6], place4 < 2)
        halves = [(line >> 1) ^ (step >> 1)]
        chosen = r ^ (step & 1)
        products(place4, chosen, lambda a: near[a] + far[a], False, halves, lhs, low, high, in_half)

    at_place(run)
    emit(low, high, 0, norm, out_ref, plain=step == 0)


def split_gradient(own, swap, relay, norm, later):
    own, swap, relay = ((x, xp, y, yp) for x, xp, y, yp in (own, swap, relay))
    _, in_half, size = own[0].shape
    out_half = own[2].shape[1]
    rows = 27 * in_half // CHUNKS
    flat = rows * 3 // 2
    part = jax.ShapeDtypeStruct((1, rows, 128), F32)
    sent = jax.ShapeDtypeStruct((flat + 2, 128), F32)
    mine = jax.ShapeDtypeStruct((flat, 128), F32)
    whole = [jax.ShapeDtypeStruct((2 * half, size), BF16) for half in (in_half, out_half)]
    lhs = pltpu.VMEM((1024, size), BF16)
    work = rows * 2 * out_half * 2 * size

    sums = [pltpu.VMEM(part.shape, F32)] * 2
    low, high, *near = call(
        near_body, [part, part, *whole, *whole], [*own, *swap], [lhs], 4 * work // 3, "near"
    )
    term, *far = call(
        functools.partial(far_body, norm),
        [sent, *whole],
        [low, high, *near[0:2], *relay],
        [lhs, *sums],
        2 * work // 3,
        "far",
    )
    term, gots, first = term.astype(jnp.float16), [], near[0]

    def rest(step, shape):
        body = functools.partial(rest_body, step, norm)
        return call(body, [shape], [first, *near[1:], *far], [lhs, *sums], 2 * work, "rest")[0]

    for step, following in ((2, 1), (1, 3)):
        term, first = lax.optimization_barrier((term, first))
        gots.append(swapped(term, 4 * step))
        term = rest(following, sent).astype(jnp.float16)
    gots.append(swapped(term, 12))
    later, first = lax.optimization_barrier((later, first))
    kept = rest(0, mine)
    out = jax.ShapeDtypeStruct((flat, 1, 128), F32)
    operands = [kept, *(got.astype(F32) for got in gots)]
    return call(sum_body, [out], operands, [], 0, "sum")[0].reshape(1, flat * 128), later


def sum_body(own, *refs):
    gots, out_ref = refs[:-1], refs[-1]
    flat = own.shape[0]
    total = own[...]
    for got in gots:
        total = total + got[0:flat, :] * jnp.exp2(-got[flat : flat + 1, :])
    out_ref[:, 0, :] = total


def any_gradient(own, swap, relay, norm):
    count = lax.axis_size(AXIS)
    half, odd, _, _ = place()

    def whole(mine, other):
        parts = jnp.concatenate([mine, other], axis=1), jnp.concatenate([other, mine], axis=1)
        return jnp.where(half == 0, *parts)

    near, next_to, far = (whole(p[0], p[1]) for p in (own, swap, relay))
    cotangent = whole(own[2], own[3])[0]
    in_half, size = own[0].shape[1:]
    far = jnp.where(at_edge(), jnp.zeros_like(far), far)
    planes = [jnp.where(odd == 0, far, next_to), near, jnp.where(odd == 0, next_to, far)]
    column = jnp.arange(size, dtype=jnp.int32) % W
    found = []
    for plane in planes:
        mine = lax.dynamic_slice_in_dim(plane[0], half * in_half, in_half, 0)
        margin = jnp.pad(mine, [(0, 0), (W + 1, W + 1)])
        for b in range(3):
            for e in range(3):
                start = W * b + e
                here = (column + e - 1 >= 0) & (column + e - 1 < W)
                shifted = jnp.where(here, margin[:, start : start + size], jnp.zeros((), mine.dtype))
                found.append(jnp.einsum("kp,op->ko", shifted, cotangent, preferred_element_type=F32))
    term = jnp.stack(found).reshape(1, -1) * norm
    both = jnp.concatenate([jnp.where(half == 0, term, 0.0), jnp.where(half == 0, 0.0, term)])
    return lax.psum_scatter(both.reshape(count, -1), AXIS, scatter_dimension=0, tiled=True)


def local(activations, weights, cotangent):
    count = lax.axis_size(AXIS)
    size = activations.shape[2]
    next_x = swapped(activations, 2)
    own_x, own_y = staged(activations, cotangent)
    next_y = swapped(own_y, 2)
    later_y, near_x = lax.optimization_barrier((own_y, next_x))
    far_x, far_y = relayed(near_x), handed(later_y)
    other_x, other_y = swapped(own_x, 1), swapped(own_y, 1)
    tables = weight_tables(weights)
    later_x, tables = lax.optimization_barrier((next_x, tables))
    next_other_x, next_other_y = swapped(later_x, 1), swapped(next_y, 1)
    far_other_x, far_other_y = swapped(far_x, 1), swapped(far_y, 1)
    own = (own_x, other_x, own_y, other_y)
    swap = (next_x, next_other_x, next_y, next_other_y)
    relay = (far_x, far_other_x, far_y, far_other_y)
    norm = 1.0 / math.sqrt(count // 2 * size)
    fits = count == 16 and activations.shape[1] == 96 and cotangent.shape[1] == 96
    xs = [part for plane in (own, swap, relay) for part in plane[:2]]
    ys = [part for plane in (own, swap, relay) for part in plane[2:]]
    forward, back = convolutions(xs, ys, tables)
    if fits:
        gradient, forward = split_gradient(own, swap, relay, norm, forward)
    else:
        gradient = any_gradient(own, swap, relay, norm)
    return forward, back, gradient


def solution(mesh):
    placed = P(("grp", AXIS), None, None)
    return jax.shard_map(
        local,
        mesh=mesh,
        in_specs=(placed, P(), placed),
        out_specs=(placed, placed, P(("grp", AXIS), None)),
        check_vma=False,
    )
```

```python
import functools
import math

import jax
import jax.numpy as jnp
from jax import lax
from jax.experimental import pallas as pl
from jax.experimental.pallas import tpu as pltpu
from jax.sharding import PartitionSpec as P

W = 64
AXIS = "slab"
F32 = jnp.float32
BF16 = jnp.bfloat16
TOP = 60000.0
CHUNKS = 8
IN_VMEM = pl.BlockSpec(memory_space=pltpu.VMEM)


def swapped(value, bit):
    count = lax.axis_size(AXIS)
    return lax.ppermute(value, AXIS, [(i, i ^ bit) for i in range(count)])


def relayed(value):
    count = lax.axis_size(AXIS)
    up = [(i, i + 4 if i + 4 < count else i + 2) for i in range(count) if not i & 2]
    down = [(i, i - 4 if i >= 4 else i - 2) for i in range(count) if i & 2]
    return lax.ppermute(value, AXIS, up + down)


def handed(value):
    count = lax.axis_size(AXIS)
    route = [i ^ 1 if i in (0, 1, count - 2, count - 1) else i + 2 if i & 2 else i - 2 for i in range(count)]
    return lax.ppermute(value, AXIS, list(enumerate(route)))


def at_edge():
    index = lax.axis_index(AXIS) >> 1
    return (index == 0) | (index == lax.axis_size(AXIS) // 2 - 1)


def place():
    index = lax.axis_index(AXIS)
    return index & 1, (index >> 1) & 1, index & 3, index >> 2


def call(body, outs, operands, scratch, flops, name):
    moved = sum(math.prod(a.shape) * a.dtype.itemsize for a in [*outs, *operands])
    return pl.pallas_call(
        body,
        out_shape=outs,
        in_specs=[IN_VMEM] * len(operands),
        out_specs=[IN_VMEM] * len(outs),
        scratch_shapes=scratch,
        cost_estimate=pl.CostEstimate(flops=flops, transcendentals=0, bytes_accessed=moved),
        compiler_params=pltpu.CompilerParams(vmem_limit_bytes=20 << 20),
        name=name,
    )(*operands)


def stage_body(x_hbm, y_hbm, x_ref, y_ref, sems):
    copies = [
        pltpu.make_async_copy(source, target, sems.at[k])
        for k, (source, target) in enumerate(((x_hbm, x_ref), (y_hbm, y_ref)))
    ]
    for copy in copies:
        copy.start()
    for copy in copies:
        copy.wait()


def staged(*arrays):
    return pl.pallas_call(
        stage_body,
        out_shape=[pltpu.VMEM(a.shape, a.dtype) for a in arrays],
        in_specs=[pl.BlockSpec(memory_space=pltpu.HBM)] * len(arrays),
        out_specs=[IN_VMEM] * len(arrays),
        scratch_shapes=[pltpu.SemaphoreType.DMA((len(arrays),))],
        name="stage",
    )(*(pltpu.with_memory_space_constraint(a, pltpu.HBM) for a in arrays))


def weight_body(w_ref, fwd_ref, back_ref):
    half, _, _, _ = place()
    chans, filters = w_ref.shape[3:]
    in_half, out_half = chans // 2, filters // 2
    start = pl.multiple_of(half * in_half, 32)
    for b in range(3):
        for e in range(3):
            block = 3 * b + e
            for a in range(3):
                turned = w_ref[a, b, e].T
                own = jnp.where(half == 0, turned[:out_half], turned[out_half:])
                fwd_ref[block * out_half : (block + 1) * out_half, a * chans : (a + 1) * chans] = own
                rows = w_ref[2 - a, 2 - b, 2 - e, pl.ds(start, in_half), :]
                back_ref[block * in_half : (block + 1) * in_half, a * filters : (a + 1) * filters] = rows


def weight_tables(weights):
    chans, filters = weights.shape[3:]
    outs = [
        jax.ShapeDtypeStruct((9 * filters // 2, 3 * chans), BF16),
        jax.ShapeDtypeStruct((9 * chans // 2, 3 * filters), BF16),
    ]
    return call(weight_body, outs, [weights], [], 0, "tables")


def fill(target, parts, half, first_row, relay=False):
    rows = parts[0].shape[1]
    for part, which in zip(parts, (half, 1 - half)):
        value = part[0]
        if relay:
            value = jnp.where(at_edge(), jnp.zeros_like(value), value)
        target[pl.ds(pl.multiple_of(first_row + which * rows, 32), rows), :] = value


def fold(product, out_ref, rows):
    size = product.shape[1]
    cell = lax.broadcasted_iota(jnp.int32, (rows, size), 1)
    column = cell % W

    def tap(b, e):
        block = 3 * b + e
        return product[block * rows : (block + 1) * rows, :]

    def over_rows(e):
        up = jnp.where(cell >= W, pltpu.roll(tap(0, e), W, 1), 0.0)
        down = jnp.where(cell < size - W, pltpu.roll(tap(2, e), size - W, 1), 0.0)
        return tap(1, e) + up + down

    left = jnp.where(column >= 1, pltpu.roll(over_rows(0), 1, 1), 0.0)
    right = jnp.where(column < W - 1, pltpu.roll(over_rows(2), size - 1, 1), 0.0)
    out_ref[0] = (over_rows(1) + left + right).astype(out_ref.dtype)


def conv_body(*refs):
    xs, ys = refs[0:6], refs[6:12]
    fwd_w, back_w, fwd_ref, back_ref, planes, product = refs[12:]
    half, odd, _, _ = place()
    for parts, table, out_ref in ((xs, fwd_w, fwd_ref), (ys, back_w, back_ref)):
        chans = 2 * parts[0].shape[1]
        for k, slot in enumerate((1, 2 - 2 * odd, 2 * odd)):
            fill(planes, parts[2 * k : 2 * k + 2], half, slot * chans, relay=k == 2)
        product[...] = jnp.dot(table[...], planes[...], preferred_element_type=F32)
        fold(product, out_ref, out_ref.shape[1])


def convolutions(xs, ys, tables):
    _, in_half, size = xs[0].shape
    out_half = ys[0].shape[1]
    outs = [
        jax.ShapeDtypeStruct((1, out_half, size), BF16),
        jax.ShapeDtypeStruct((1, in_half, size), BF16),
    ]
    scratch = [pltpu.VMEM((6 * in_half, size), BF16), pltpu.VMEM((9 * out_half, size), F32)]
    flops = 2 * 2 * 54 * in_half * out_half * size
    return call(conv_body, outs, [*xs, *ys, *tables], scratch, flops, "convolve")


def pieces(chunk, chunks, in_half):
    rows = 27 * in_half // chunks
    at, end, found = chunk * rows, (chunk + 1) * rows, []
    while at < end:
        tap, first = divmod(at, in_half)
        count = min(in_half - first, end - at)
        found.append((tap, first, count, at - chunk * rows))
        at += count
    return found


def moved(plane, b, e, cells):
    size = plane.shape[1]
    step = W * (b - 1) + e - 1
    if step:
        plane = pltpu.roll(plane, -step % size, 1)
    keep = None
    if b == 0:
        keep = cells >= W
    if b == 2:
        keep = cells < size - W
    if e != 1:
        inside = cells % W >= 1 if e == 0 else cells % W < W - 1
        keep = inside if keep is None else keep & inside
    return plane if keep is None else plane * keep.astype(F32).astype(plane.dtype)


def products(place4, r, pairs_of, accumulate, halves, lhs, low, high, in_half):
    for a in range(3):
        pairs = pairs_of(a)
        rows = []
        for tap, first, count, row in pieces(place4 + 4 * r, CHUNKS, in_half):
            if tap // 9 == a:
                begin, end = first // 16 * 16, -(-(first + count) // 16) * 16
                rows += [(k, tap, first, count, row, begin, end) for k in range(len(halves))]
        if not rows or not pairs:
            continue
        total = None
        for x_ref, y_ref in pairs:
            size = x_ref.shape[1]
            cells = lax.broadcasted_iota(jnp.int32, (1, size), 1)
            at = 0
            for k, tap, first, count, row, begin, end in rows:
                start = pl.multiple_of(halves[k] * in_half + begin, 16)
                source = x_ref[pl.ds(start, end - begin), :]
                lhs[at : at + end - begin, :] = moved(source, tap // 3 % 3, tap % 3, cells)
                at += end - begin
            term = lax.dot_general(
                lhs[0:at, :], y_ref[...], (((1,), (1,)), ((), ())), preferred_element_type=F32
            )
            total = term if total is None else total + term
        at = 0
        for k, tap, first, count, row, begin, end in rows:
            got = total[at + first - begin : at + first - begin + count]
            at += end - begin
            where = slice(row, row + count)
            if accumulate:
                low[k, where, :] += got[:, :128]
                high[k, where, 0:64] += got[:, 128:]
            else:
                low[k, where, :] = got[:, :128]
                high[k, where, 0:64] = got[:, 128:]


def at_place(run):
    _, _, mine, line = place()
    for place4 in range(4):
        for r in range(2):
            pl.when((mine == place4) & ((line & 1) == r))(functools.partial(run, place4, r))


def pairs_for(own, swap, far, even):
    (xo, yo), (xs, ys), (xf, yf) = own, swap, far
    lower, upper = ((xo, yo), (xs, ys)) if even else ((xs, ys), (xo, yo))
    near = ([(lower[0], upper[1])], [lower, upper], [(upper[0], lower[1])])
    first, last = [(xf, yo)], [(xo, yf)]
    return near, (first if even else last, [], last if even else first)


def near_body(xo, xop, yo, yop, xs, xsp, ys, ysp, low, high, *rest):
    fulls, lhs = rest[0:4], rest[4]
    half, _, _, line = place()
    for full, parts in zip(fulls, ((xo, xop), (yo, yop), (xs, xsp), (ys, ysp))):
        fill(full, parts, half, 0)
    high[...] = jnp.zeros_like(high)

    def run(place4, r):
        near, _ = pairs_for(fulls[0:2], fulls[2:4], (None, None), place4 < 2)
        products(place4, r, lambda a: near[a], False, [(line >> 1) ^ 1], lhs, low, high, xo.shape[1])

    at_place(run)


def emit(low, high, row, norm, out, plain=False):
    count = low.shape[1] // 2
    if plain:
        by = norm
    else:
        top = jnp.maximum(jnp.max(jnp.abs(low[row])), jnp.max(jnp.abs(high[row])))
        top = jnp.maximum(jnp.broadcast_to(top, (8, 128)) * norm, 1e-25)
        power = jnp.floor(jnp.log(TOP / top) * (1.0 / math.log(2.0)))
        out[3 * count : 3 * count + 2, :] = power[0:2]
        by = jnp.exp2(power)[0:1] * norm
    left = lax.broadcasted_iota(jnp.int32, (count, 128), 1) < 64
    even_low = low[row, pl.ds(0, count, stride=2), :]
    odd_low = pltpu.roll(low[row, pl.ds(1, count, stride=2), :], 64, 1)
    even_high = high[row, pl.ds(0, count, stride=2), :]
    odd_high = pltpu.roll(high[row, pl.ds(1, count, stride=2), :], 64, 1)
    out[pl.ds(0, count, stride=3), :] = even_low * by
    out[pl.ds(1, count, stride=3), :] = jnp.where(left, even_high, odd_low) * by
    out[pl.ds(2, count, stride=3), :] = jnp.where(left, odd_low, odd_high) * by


def far_body(norm, low_in, high_in, xof, yof, xr, xrp, yr, yrp, out_ref, xrf, yrf, lhs, low, high):
    half, _, _, line = place()
    fill(xrf, (xr, xrp), half, 0, relay=True)
    fill(yrf, (yr, yrp), half, 0, relay=True)
    low[...] = low_in[...]
    high[...] = high_in[...]

    def run(place4, r):
        _, far = pairs_for((xof, yof), (None, None), (xrf, yrf), place4 < 2)
        products(place4, r, lambda a: far[a], True, [(line >> 1) ^ 1], lhs, low, high, xr.shape[1])

    at_place(run)
    emit(low, high, 0, norm, out_ref)


def rest_body(step, norm, *refs):
    fulls, (out_ref, lhs, low, high) = refs[0:6], refs[6:]
    _, _, _, line = place()
    in_half = fulls[0].shape[0] // 2
    high[...] = jnp.zeros_like(high)

    def run(place4, r):
        near, far = pairs_for(fulls[0:2], fulls[2:4], fulls[4:6], place4 < 2)
        halves = [(line >> 1) ^ (step >> 1)]
        chosen = r ^ (step & 1)
        products(place4, chosen, lambda a: near[a] + far[a], False, halves, lhs, low, high, in_half)

    at_place(run)
    emit(low, high, 0, norm, out_ref, plain=step == 0)


def split_gradient(own, swap, relay, norm, later):
    own, swap, relay = ((x, xp, y, yp) for x, xp, y, yp in (own, swap, relay))
    _, in_half, size = own[0].shape
    out_half = own[2].shape[1]
    rows = 27 * in_half // CHUNKS
    flat = rows * 3 // 2
    part = jax.ShapeDtypeStruct((1, rows, 128), F32)
    sent = jax.ShapeDtypeStruct((flat + 2, 128), F32)
    mine = jax.ShapeDtypeStruct((flat, 128), F32)
    whole = [jax.ShapeDtypeStruct((2 * half, size), BF16) for half in (in_half, out_half)]
    lhs = pltpu.VMEM((1024, size), BF16)
    work = rows * 2 * out_half * 2 * size

    sums = [pltpu.VMEM(part.shape, F32)] * 2
    low, high, *near = call(
        near_body, [part, part, *whole, *whole], [*own, *swap], [lhs], 4 * work // 3, "near"
    )
    term, *far = call(
        functools.partial(far_body, norm),
        [sent, *whole],
        [low, high, *near[0:2], *relay],
        [lhs, *sums],
        2 * work // 3,
        "far",
    )
    term, gots, first = term.astype(jnp.float16), [], near[0]

    def rest(step, shape):
        body = functools.partial(rest_body, step, norm)
        return call(body, [shape], [first, *near[1:], *far], [lhs, *sums], 2 * work, "rest")[0]

    for step, following in ((2, 1), (1, 3)):
        term, first = lax.optimization_barrier((term, first))
        gots.append(swapped(term, 4 * step))
        term = rest(following, sent).astype(jnp.float16)
    gots.append(swapped(term, 12))
    later, first = lax.optimization_barrier((later, first))
    kept = rest(0, mine)
    out = jax.ShapeDtypeStruct((flat, 1, 128), F32)
    operands = [kept, *(got.astype(F32) for got in gots)]
    return call(sum_body, [out], operands, [], 0, "sum")[0].reshape(1, flat * 128), later


def sum_body(own, *refs):
    gots, out_ref = refs[:-1], refs[-1]
    flat = own.shape[0]
    total = own[...]
    for got in gots:
        total = total + got[0:flat, :] * jnp.exp2(-got[flat : flat + 1, :])
    out_ref[:, 0, :] = total


def any_gradient(own, swap, relay, norm):
    count = lax.axis_size(AXIS)
    half, odd, _, _ = place()

    def whole(mine, other):
        parts = jnp.concatenate([mine, other], axis=1), jnp.concatenate([other, mine], axis=1)
        return jnp.where(half == 0, *parts)

    near, next_to, far = (whole(p[0], p[1]) for p in (own, swap, relay))
    cotangent = whole(own[2], own[3])[0]
    in_half, size = own[0].shape[1:]
    far = jnp.where(at_edge(), jnp.zeros_like(far), far)
    planes = [jnp.where(odd == 0, far, next_to), near, jnp.where(odd == 0, next_to, far)]
    column = jnp.arange(size, dtype=jnp.int32) % W
    found = []
    for plane in planes:
        mine = lax.dynamic_slice_in_dim(plane[0], half * in_half, in_half, 0)
        margin = jnp.pad(mine, [(0, 0), (W + 1, W + 1)])
        for b in range(3):
            for e in range(3):
                start = W * b + e
                here = (column + e - 1 >= 0) & (column + e - 1 < W)
                shifted = jnp.where(here, margin[:, start : start + size], jnp.zeros((), mine.dtype))
                found.append(jnp.einsum("kp,op->ko", shifted, cotangent, preferred_element_type=F32))
    term = jnp.stack(found).reshape(1, -1) * norm
    both = jnp.concatenate([jnp.where(half == 0, term, 0.0), jnp.where(half == 0, 0.0, term)])
    return lax.psum_scatter(both.reshape(count, -1), AXIS, scatter_dimension=0, tiled=True)


def local(activations, weights, cotangent):
    count = lax.axis_size(AXIS)
    size = activations.shape[2]
    next_x = swapped(activations, 2)
    own_x, own_y = staged(activations, cotangent)
    next_y = swapped(own_y, 2)
    later_y, near_x = lax.optimization_barrier((own_y, next_x))
    far_x, far_y = relayed(near_x), handed(later_y)
    other_x = swapped(own_x, 1)
    tables = weight_tables(weights)
    later_own, tables = lax.optimization_barrier((own_y, tables))
    other_y = swapped(later_own, 1)
    next_other_x, next_other_y = swapped(next_x, 1), swapped(next_y, 1)
    far_other_x, far_other_y = swapped(far_x, 1), swapped(far_y, 1)
    own = (own_x, other_x, own_y, other_y)
    swap = (next_x, next_other_x, next_y, next_other_y)
    relay = (far_x, far_other_x, far_y, far_other_y)
    norm = 1.0 / math.sqrt(count // 2 * size)
    fits = count == 16 and activations.shape[1] == 96 and cotangent.shape[1] == 96
    xs = [part for plane in (own, swap, relay) for part in plane[:2]]
    ys = [part for plane in (own, swap, relay) for part in plane[2:]]
    forward, back = convolutions(xs, ys, tables)
    if fits:
        gradient, forward = split_gradient(own, swap, relay, norm, forward)
    else:
        gradient = any_gradient(own, swap, relay, norm)
    return forward, back, gradient


def solution(mesh):
    placed = P(("grp", AXIS), None, None)
    return jax.shard_map(
        local,
        mesh=mesh,
        in_specs=(placed, P(), placed),
        out_specs=(placed, placed, P(("grp", AXIS), None)),
        check_vma=False,
    )
```

```python
import functools
import math

import jax
import jax.numpy as jnp
from jax import lax
from jax.experimental import pallas as pl
from jax.experimental.pallas import tpu as pltpu
from jax.sharding import PartitionSpec as P

W = 64
AXIS = "slab"
F32 = jnp.float32
BF16 = jnp.bfloat16
TOP = 60000.0
CHUNKS = 8
IN_VMEM = pl.BlockSpec(memory_space=pltpu.VMEM)


def swapped(value, bit):
    count = lax.axis_size(AXIS)
    return lax.ppermute(value, AXIS, [(i, i ^ bit) for i in range(count)])


def relayed(value):
    count = lax.axis_size(AXIS)
    up = [(i, i + 4 if i + 4 < count else i + 2) for i in range(count) if not i & 2]
    down = [(i, i - 4 if i >= 4 else i - 2) for i in range(count) if i & 2]
    return lax.ppermute(value, AXIS, up + down)


def handed(value):
    count = lax.axis_size(AXIS)
    route = [i ^ 1 if i in (0, 1, count - 2, count - 1) else i + 2 if i & 2 else i - 2 for i in range(count)]
    return lax.ppermute(value, AXIS, list(enumerate(route)))


def at_edge():
    index = lax.axis_index(AXIS) >> 1
    return (index == 0) | (index == lax.axis_size(AXIS) // 2 - 1)


def place():
    index = lax.axis_index(AXIS)
    return index & 1, (index >> 1) & 1, index & 3, index >> 2


def call(body, outs, operands, scratch, flops, name, aliases=()):
    moved = sum(math.prod(a.shape) * a.dtype.itemsize for a in [*outs, *operands])
    return pl.pallas_call(
        body,
        out_shape=outs,
        in_specs=[IN_VMEM] * len(operands),
        out_specs=[IN_VMEM] * len(outs),
        scratch_shapes=scratch,
        input_output_aliases=dict(aliases),
        cost_estimate=pl.CostEstimate(flops=flops, transcendentals=0, bytes_accessed=moved),
        compiler_params=pltpu.CompilerParams(vmem_limit_bytes=20 << 20),
        name=name,
    )(*operands)


def stage_body(x_hbm, y_hbm, x_ref, y_ref, sems):
    copies = [
        pltpu.make_async_copy(source, target, sems.at[k])
        for k, (source, target) in enumerate(((x_hbm, x_ref), (y_hbm, y_ref)))
    ]
    for copy in copies:
        copy.start()
    for copy in copies:
        copy.wait()


def staged(*arrays):
    return pl.pallas_call(
        stage_body,
        out_shape=[pltpu.VMEM(a.shape, a.dtype) for a in arrays],
        in_specs=[pl.BlockSpec(memory_space=pltpu.HBM)] * len(arrays),
        out_specs=[IN_VMEM] * len(arrays),
        scratch_shapes=[pltpu.SemaphoreType.DMA((len(arrays),))],
        name="stage",
    )(*(pltpu.with_memory_space_constraint(a, pltpu.HBM) for a in arrays))


def weight_body(w_ref, fwd_ref, back_ref):
    half, _, _, _ = place()
    chans, filters = w_ref.shape[3:]
    in_half, out_half = chans // 2, filters // 2
    start = pl.multiple_of(half * in_half, 32)
    for b in range(3):
        for e in range(3):
            block = 3 * b + e
            for a in range(3):
                turned = w_ref[a, b, e].T
                own = jnp.where(half == 0, turned[:out_half], turned[out_half:])
                fwd_ref[block * out_half : (block + 1) * out_half, a * chans : (a + 1) * chans] = own
                rows = w_ref[2 - a, 2 - b, 2 - e, pl.ds(start, in_half), :]
                back_ref[block * in_half : (block + 1) * in_half, a * filters : (a + 1) * filters] = rows


def weight_tables(weights):
    chans, filters = weights.shape[3:]
    outs = [
        jax.ShapeDtypeStruct((9 * filters // 2, 3 * chans), BF16),
        jax.ShapeDtypeStruct((9 * chans // 2, 3 * filters), BF16),
    ]
    return call(weight_body, outs, [weights], [], 0, "tables")


def fill(target, parts, half, first_row, relay=False):
    rows = parts[0].shape[1]
    for part, which in zip(parts, (half, 1 - half)):
        value = part[0]
        if relay:
            value = jnp.where(at_edge(), jnp.zeros_like(value), value)
        target[pl.ds(pl.multiple_of(first_row + which * rows, 32), rows), :] = value


def fold(product, out_ref, rows):
    size = product.shape[1]
    cell = lax.broadcasted_iota(jnp.int32, (rows, size), 1)
    column = cell % W

    def tap(b, e):
        block = 3 * b + e
        return product[block * rows : (block + 1) * rows, :]

    def over_rows(e):
        up = jnp.where(cell >= W, pltpu.roll(tap(0, e), W, 1), 0.0)
        down = jnp.where(cell < size - W, pltpu.roll(tap(2, e), size - W, 1), 0.0)
        return tap(1, e) + up + down

    left = jnp.where(column >= 1, pltpu.roll(over_rows(0), 1, 1), 0.0)
    right = jnp.where(column < W - 1, pltpu.roll(over_rows(2), size - 1, 1), 0.0)
    out_ref[0] = (over_rows(1) + left + right).astype(out_ref.dtype)


def conv_body(*refs):
    xs, ys = refs[0:6], refs[6:12]
    fwd_w, back_w, fwd_ref, back_ref, planes, product = refs[12:]
    half, odd, _, _ = place()
    for parts, table, out_ref in ((xs, fwd_w, fwd_ref), (ys, back_w, back_ref)):
        chans = 2 * parts[0].shape[1]
        for k, slot in enumerate((1, 2 - 2 * odd, 2 * odd)):
            fill(planes, parts[2 * k : 2 * k + 2], half, slot * chans, relay=k == 2)
        product[...] = jnp.dot(table[...], planes[...], preferred_element_type=F32)
        fold(product, out_ref, out_ref.shape[1])


def convolutions(xs, ys, tables):
    _, in_half, size = xs[0].shape
    out_half = ys[0].shape[1]
    outs = [
        jax.ShapeDtypeStruct((1, out_half, size), BF16),
        jax.ShapeDtypeStruct((1, in_half, size), BF16),
    ]
    scratch = [pltpu.VMEM((6 * in_half, size), BF16), pltpu.VMEM((9 * out_half, size), F32)]
    flops = 2 * 2 * 54 * in_half * out_half * size
    return call(conv_body, outs, [*xs, *ys, *tables], scratch, flops, "convolve")


def pieces(chunk, chunks, in_half):
    rows = 27 * in_half // chunks
    at, end, found = chunk * rows, (chunk + 1) * rows, []
    while at < end:
        tap, first = divmod(at, in_half)
        count = min(in_half - first, end - at)
        found.append((tap, first, count, at - chunk * rows))
        at += count
    return found


def moved(plane, b, e, cells):
    size = plane.shape[1]
    step = W * (b - 1) + e - 1
    if step:
        plane = pltpu.roll(plane, -step % size, 1)
    keep = None
    if b == 0:
        keep = cells >= W
    if b == 2:
        keep = cells < size - W
    if e != 1:
        inside = cells % W >= 1 if e == 0 else cells % W < W - 1
        keep = inside if keep is None else keep & inside
    return plane if keep is None else plane * keep.astype(F32).astype(plane.dtype)


def products(place4, r, pairs_of, accumulate, halves, lhs, low, high, in_half):
    for a in range(3):
        pairs = pairs_of(a)
        rows = []
        for tap, first, count, row in pieces(place4 + 4 * r, CHUNKS, in_half):
            if tap // 9 == a:
                begin, end = first // 16 * 16, -(-(first + count) // 16) * 16
                rows += [(k, tap, first, count, row, begin, end) for k in range(len(halves))]
        if not rows or not pairs:
            continue
        total = None
        for x_ref, y_ref in pairs:
            size = x_ref.shape[1]
            cells = lax.broadcasted_iota(jnp.int32, (1, size), 1)
            at = 0
            for k, tap, first, count, row, begin, end in rows:
                start = pl.multiple_of(halves[k] * in_half + begin, 16)
                source = x_ref[pl.ds(start, end - begin), :]
                lhs[at : at + end - begin, :] = moved(source, tap // 3 % 3, tap % 3, cells)
                at += end - begin
            term = lax.dot_general(
                lhs[0:at, :], y_ref[...], (((1,), (1,)), ((), ())), preferred_element_type=F32
            )
            total = term if total is None else total + term
        at = 0
        for k, tap, first, count, row, begin, end in rows:
            got = total[at + first - begin : at + first - begin + count]
            at += end - begin
            where = slice(row, row + count)
            if accumulate:
                low[k, where, :] += got[:, :128]
                high[k, where, 0:64] += got[:, 128:]
            else:
                low[k, where, :] = got[:, :128]
                high[k, where, 0:64] = got[:, 128:]


def at_place(run):
    _, _, mine, line = place()
    for place4 in range(4):
        for r in range(2):
            pl.when((mine == place4) & ((line & 1) == r))(functools.partial(run, place4, r))


def pairs_for(own, swap, far, even):
    (xo, yo), (xs, ys), (xf, yf) = own, swap, far
    lower, upper = ((xo, yo), (xs, ys)) if even else ((xs, ys), (xo, yo))
    near = ([(lower[0], upper[1])], [lower, upper], [(upper[0], lower[1])])
    first, last = [(xf, yo)], [(xo, yf)]
    return near, (first if even else last, [], last if even else first)


def near_body(xo, xop, yo, yop, xs, xsp, ys, ysp, low, high, *rest):
    fulls, lhs = rest[0:4], rest[4]
    half, _, _, line = place()
    for full, parts in zip(fulls, ((xo, xop), (yo, yop), (xs, xsp), (ys, ysp))):
        fill(full, parts, half, 0)
    high[...] = jnp.zeros_like(high)

    def run(place4, r):
        near, _ = pairs_for(fulls[0:2], fulls[2:4], (None, None), place4 < 2)
        products(place4, r, lambda a: near[a], False, [(line >> 1) ^ 1], lhs, low, high, xo.shape[1])

    at_place(run)


def emit(low, high, row, norm, out, plain=False):
    count = low.shape[1] // 2
    if plain:
        by = norm
    else:
        top = jnp.maximum(jnp.max(jnp.abs(low[row])), jnp.max(jnp.abs(high[row])))
        top = jnp.maximum(jnp.broadcast_to(top, (8, 128)) * norm, 1e-25)
        power = jnp.floor(jnp.log(TOP / top) * (1.0 / math.log(2.0)))
        out[3 * count : 3 * count + 2, :] = power[0:2]
        by = jnp.exp2(power)[0:1] * norm
    left = lax.broadcasted_iota(jnp.int32, (count, 128), 1) < 64
    even_low = low[row, pl.ds(0, count, stride=2), :]
    odd_low = pltpu.roll(low[row, pl.ds(1, count, stride=2), :], 64, 1)
    even_high = high[row, pl.ds(0, count, stride=2), :]
    odd_high = pltpu.roll(high[row, pl.ds(1, count, stride=2), :], 64, 1)
    out[pl.ds(0, count, stride=3), :] = even_low * by
    out[pl.ds(1, count, stride=3), :] = jnp.where(left, even_high, odd_low) * by
    out[pl.ds(2, count, stride=3), :] = jnp.where(left, odd_low, odd_high) * by


def far_body(norm, low_in, high_in, xof, yof, xr, xrp, yr, yrp, out_ref, xrf, yrf, low, high, lhs):
    half, _, _, line = place()
    fill(xrf, (xr, xrp), half, 0, relay=True)
    fill(yrf, (yr, yrp), half, 0, relay=True)

    def run(place4, r):
        _, far = pairs_for((xof, yof), (None, None), (xrf, yrf), place4 < 2)
        products(place4, r, lambda a: far[a], True, [(line >> 1) ^ 1], lhs, low, high, xr.shape[1])

    at_place(run)
    emit(low, high, 0, norm, out_ref)


def rest_body(step, norm, *refs):
    fulls, (out_ref, lhs, low, high) = refs[0:6], refs[6:]
    _, _, _, line = place()
    in_half = fulls[0].shape[0] // 2
    high[...] = jnp.zeros_like(high)

    def run(place4, r):
        near, far = pairs_for(fulls[0:2], fulls[2:4], fulls[4:6], place4 < 2)
        halves = [(line >> 1) ^ (step >> 1)]
        chosen = r ^ (step & 1)
        products(place4, chosen, lambda a: near[a] + far[a], False, halves, lhs, low, high, in_half)

    at_place(run)
    emit(low, high, 0, norm, out_ref, plain=step == 0)


def split_gradient(own, swap, relay, norm, later):
    own, swap, relay = ((x, xp, y, yp) for x, xp, y, yp in (own, swap, relay))
    _, in_half, size = own[0].shape
    out_half = own[2].shape[1]
    rows = 27 * in_half // CHUNKS
    flat = rows * 3 // 2
    part = jax.ShapeDtypeStruct((1, rows, 128), F32)
    sent = jax.ShapeDtypeStruct((flat + 2, 128), F32)
    mine = jax.ShapeDtypeStruct((flat, 128), F32)
    whole = [jax.ShapeDtypeStruct((2 * half, size), BF16) for half in (in_half, out_half)]
    lhs = pltpu.VMEM((1024, size), BF16)
    work = rows * 2 * out_half * 2 * size

    sums = [pltpu.VMEM(part.shape, F32)] * 2
    low, high, *near = call(
        near_body, [part, part, *whole, *whole], [*own, *swap], [lhs], 4 * work // 3, "near"
    )
    term, *far, _, _ = call(
        functools.partial(far_body, norm),
        [sent, *whole, part, part],
        [low, high, *near[0:2], *relay],
        [lhs],
        2 * work // 3,
        "far",
        ((0, 3), (1, 4)),
    )
    term, gots, first = term.astype(jnp.float16), [], near[0]

    def rest(step, shape):
        body = functools.partial(rest_body, step, norm)
        return call(body, [shape], [first, *near[1:], *far], [lhs, *sums], 2 * work, "rest")[0]

    for step, following in ((2, 1), (1, 3)):
        term, first = lax.optimization_barrier((term, first))
        gots.append(swapped(term, 4 * step))
        term = rest(following, sent).astype(jnp.float16)
    gots.append(swapped(term, 12))
    later, first = lax.optimization_barrier((later, first))
    kept = rest(0, mine)
    out = jax.ShapeDtypeStruct((flat, 1, 128), F32)
    operands = [kept, *(got.astype(F32) for got in gots)]
    return call(sum_body, [out], operands, [], 0, "sum")[0].reshape(1, flat * 128), later


def sum_body(own, *refs):
    gots, out_ref = refs[:-1], refs[-1]
    flat = own.shape[0]
    total = own[...]
    for got in gots:
        total = total + got[0:flat, :] * jnp.exp2(-got[flat : flat + 1, :])
    out_ref[:, 0, :] = total


def any_gradient(own, swap, relay, norm):
    count = lax.axis_size(AXIS)
    half, odd, _, _ = place()

    def whole(mine, other):
        parts = jnp.concatenate([mine, other], axis=1), jnp.concatenate([other, mine], axis=1)
        return jnp.where(half == 0, *parts)

    near, next_to, far = (whole(p[0], p[1]) for p in (own, swap, relay))
    cotangent = whole(own[2], own[3])[0]
    in_half, size = own[0].shape[1:]
    far = jnp.where(at_edge(), jnp.zeros_like(far), far)
    planes = [jnp.where(odd == 0, far, next_to), near, jnp.where(odd == 0, next_to, far)]
    column = jnp.arange(size, dtype=jnp.int32) % W
    found = []
    for plane in planes:
        mine = lax.dynamic_slice_in_dim(plane[0], half * in_half, in_half, 0)
        margin = jnp.pad(mine, [(0, 0), (W + 1, W + 1)])
        for b in range(3):
            for e in range(3):
                start = W * b + e
                here = (column + e - 1 >= 0) & (column + e - 1 < W)
                shifted = jnp.where(here, margin[:, start : start + size], jnp.zeros((), mine.dtype))
                found.append(jnp.einsum("kp,op->ko", shifted, cotangent, preferred_element_type=F32))
    term = jnp.stack(found).reshape(1, -1) * norm
    both = jnp.concatenate([jnp.where(half == 0, term, 0.0), jnp.where(half == 0, 0.0, term)])
    return lax.psum_scatter(both.reshape(count, -1), AXIS, scatter_dimension=0, tiled=True)


def local(activations, weights, cotangent):
    count = lax.axis_size(AXIS)
    size = activations.shape[2]
    next_x = swapped(activations, 2)
    own_x, own_y = staged(activations, cotangent)
    next_y = swapped(own_y, 2)
    later_y, near_x = lax.optimization_barrier((own_y, next_x))
    far_x, far_y = relayed(near_x), handed(later_y)
    other_x = swapped(own_x, 1)
    tables = weight_tables(weights)
    later_own, tables = lax.optimization_barrier((own_y, tables))
    other_y = swapped(later_own, 1)
    next_other_x, next_other_y = swapped(next_x, 1), swapped(next_y, 1)
    far_other_x, far_other_y = swapped(far_x, 1), swapped(far_y, 1)
    own = (own_x, other_x, own_y, other_y)
    swap = (next_x, next_other_x, next_y, next_other_y)
    relay = (far_x, far_other_x, far_y, far_other_y)
    norm = 1.0 / math.sqrt(count // 2 * size)
    fits = count == 16 and activations.shape[1] == 96 and cotangent.shape[1] == 96
    xs = [part for plane in (own, swap, relay) for part in plane[:2]]
    ys = [part for plane in (own, swap, relay) for part in plane[2:]]
    forward, back = convolutions(xs, ys, tables)
    if fits:
        gradient, forward = split_gradient(own, swap, relay, norm, forward)
    else:
        gradient = any_gradient(own, swap, relay, norm)
    return forward, back, gradient


def solution(mesh):
    placed = P(("grp", AXIS), None, None)
    return jax.shard_map(
        local,
        mesh=mesh,
        in_specs=(placed, P(), placed),
        out_specs=(placed, placed, P(("grp", AXIS), None)),
        check_vma=False,
    )
```

```python
import functools
import math

import jax
import jax.numpy as jnp
from jax import lax
from jax.experimental import pallas as pl
from jax.experimental.pallas import tpu as pltpu
from jax.sharding import PartitionSpec as P

W = 64
AXIS = "slab"
F32 = jnp.float32
BF16 = jnp.bfloat16
TOP = 60000.0
CHUNKS = 8
IN_VMEM = pl.BlockSpec(memory_space=pltpu.VMEM)


def swapped(value, bit):
    count = lax.axis_size(AXIS)
    return lax.ppermute(value, AXIS, [(i, i ^ bit) for i in range(count)])


def relayed(value):
    count = lax.axis_size(AXIS)
    up = [(i, i + 4 if i + 4 < count else i + 2) for i in range(count) if not i & 2]
    down = [(i, i - 4 if i >= 4 else i - 2) for i in range(count) if i & 2]
    return lax.ppermute(value, AXIS, up + down)


def handed(value):
    count = lax.axis_size(AXIS)
    route = [i ^ 1 if i in (0, 1, count - 2, count - 1) else i + 2 if i & 2 else i - 2 for i in range(count)]
    return lax.ppermute(value, AXIS, list(enumerate(route)))


def at_edge():
    index = lax.axis_index(AXIS) >> 1
    return (index == 0) | (index == lax.axis_size(AXIS) // 2 - 1)


def place():
    index = lax.axis_index(AXIS)
    return index & 1, (index >> 1) & 1, index & 3, index >> 2


def call(body, outs, operands, scratch, flops, name):
    moved = sum(math.prod(a.shape) * a.dtype.itemsize for a in [*outs, *operands])
    return pl.pallas_call(
        body,
        out_shape=outs,
        in_specs=[IN_VMEM] * len(operands),
        out_specs=[IN_VMEM] * len(outs),
        scratch_shapes=scratch,
        cost_estimate=pl.CostEstimate(flops=flops, transcendentals=0, bytes_accessed=moved),
        compiler_params=pltpu.CompilerParams(vmem_limit_bytes=20 << 20),
        name=name,
    )(*operands)


def stage_body(x_hbm, y_hbm, x_ref, y_ref, sems):
    copies = [
        pltpu.make_async_copy(source, target, sems.at[k])
        for k, (source, target) in enumerate(((x_hbm, x_ref), (y_hbm, y_ref)))
    ]
    for copy in copies:
        copy.start()
    for copy in copies:
        copy.wait()


def staged(*arrays):
    return pl.pallas_call(
        stage_body,
        out_shape=[pltpu.VMEM(a.shape, a.dtype) for a in arrays],
        in_specs=[pl.BlockSpec(memory_space=pltpu.HBM)] * len(arrays),
        out_specs=[IN_VMEM] * len(arrays),
        scratch_shapes=[pltpu.SemaphoreType.DMA((len(arrays),))],
        name="stage",
    )(*(pltpu.with_memory_space_constraint(a, pltpu.HBM) for a in arrays))


def weight_body(w_ref, fwd_ref, back_ref):
    half, _, _, _ = place()
    chans, filters = w_ref.shape[3:]
    in_half, out_half = chans // 2, filters // 2
    start = pl.multiple_of(half * in_half, 32)
    for b in range(3):
        for e in range(3):
            block = 3 * b + e
            for a in range(3):
                turned = w_ref[a, b, e].T
                own = jnp.where(half == 0, turned[:out_half], turned[out_half:])
                fwd_ref[block * out_half : (block + 1) * out_half, a * chans : (a + 1) * chans] = own
                rows = w_ref[2 - a, 2 - b, 2 - e, pl.ds(start, in_half), :]
                back_ref[block * in_half : (block + 1) * in_half, a * filters : (a + 1) * filters] = rows


def weight_tables(weights):
    chans, filters = weights.shape[3:]
    outs = [
        jax.ShapeDtypeStruct((9 * filters // 2, 3 * chans), BF16),
        jax.ShapeDtypeStruct((9 * chans // 2, 3 * filters), BF16),
    ]
    return call(weight_body, outs, [weights], [], 0, "tables")


def fill(target, parts, half, first_row, relay=False):
    rows = parts[0].shape[1]
    for part, which in zip(parts, (half, 1 - half)):
        value = part[0]
        if relay:
            value = jnp.where(at_edge(), jnp.zeros_like(value), value)
        target[pl.ds(pl.multiple_of(first_row + which * rows, 32), rows), :] = value


def fold(product, out_ref, rows):
    size = product.shape[1]
    cell = lax.broadcasted_iota(jnp.int32, (rows, size), 1)
    column = cell % W

    def tap(b, e):
        block = 3 * b + e
        return product[block * rows : (block + 1) * rows, :]

    def over_rows(e):
        up = jnp.where(cell >= W, pltpu.roll(tap(0, e), W, 1), 0.0)
        down = jnp.where(cell < size - W, pltpu.roll(tap(2, e), size - W, 1), 0.0)
        return tap(1, e) + up + down

    left = jnp.where(column >= 1, pltpu.roll(over_rows(0), 1, 1), 0.0)
    right = jnp.where(column < W - 1, pltpu.roll(over_rows(2), size - 1, 1), 0.0)
    out_ref[0] = (over_rows(1) + left + right).astype(out_ref.dtype)


def conv_body(*refs):
    xs, ys = refs[0:6], refs[6:12]
    fwd_w, back_w, fwd_ref, back_ref, planes, product = refs[12:]
    half, odd, _, _ = place()
    for parts, table, out_ref in ((xs, fwd_w, fwd_ref), (ys, back_w, back_ref)):
        chans = 2 * parts[0].shape[1]
        for k, slot in enumerate((1, 2 - 2 * odd, 2 * odd)):
            fill(planes, parts[2 * k : 2 * k + 2], half, slot * chans, relay=k == 2)
        product[...] = jnp.dot(table[...], planes[...], preferred_element_type=F32)
        fold(product, out_ref, out_ref.shape[1])


def convolutions(xs, ys, tables):
    _, in_half, size = xs[0].shape
    out_half = ys[0].shape[1]
    outs = [
        jax.ShapeDtypeStruct((1, out_half, size), BF16),
        jax.ShapeDtypeStruct((1, in_half, size), BF16),
    ]
    scratch = [pltpu.VMEM((6 * in_half, size), BF16), pltpu.VMEM((9 * out_half, size), F32)]
    flops = 2 * 2 * 54 * in_half * out_half * size
    return call(conv_body, outs, [*xs, *ys, *tables], scratch, flops, "convolve")


def pieces(chunk, chunks, in_half):
    rows = 27 * in_half // chunks
    at, end, found = chunk * rows, (chunk + 1) * rows, []
    while at < end:
        tap, first = divmod(at, in_half)
        count = min(in_half - first, end - at)
        found.append((tap, first, count, at - chunk * rows))
        at += count
    return found


def moved(plane, b, e, cells):
    size = plane.shape[1]
    step = W * (b - 1) + e - 1
    if step:
        plane = pltpu.roll(plane, -step % size, 1)
    keep = None
    if b == 0:
        keep = cells >= W
    if b == 2:
        keep = cells < size - W
    if e != 1:
        inside = cells % W >= 1 if e == 0 else cells % W < W - 1
        keep = inside if keep is None else keep & inside
    return plane if keep is None else plane * keep.astype(F32).astype(plane.dtype)


def products(place4, r, pairs_of, accumulate, halves, lhs, low, high, in_half):
    for a in range(3):
        pairs = pairs_of(a)
        rows = []
        for tap, first, count, row in pieces(place4 + 4 * r, CHUNKS, in_half):
            if tap // 9 == a:
                begin, end = first // 16 * 16, -(-(first + count) // 16) * 16
                rows += [(k, tap, first, count, row, begin, end) for k in range(len(halves))]
        if not rows or not pairs:
            continue
        total = None
        for x_ref, y_ref in pairs:
            size = x_ref.shape[1]
            cells = lax.broadcasted_iota(jnp.int32, (1, size), 1)
            at = 0
            for k, tap, first, count, row, begin, end in rows:
                start = pl.multiple_of(halves[k] * in_half + begin, 16)
                source = x_ref[pl.ds(start, end - begin), :]
                lhs[at : at + end - begin, :] = moved(source, tap // 3 % 3, tap % 3, cells)
                at += end - begin
            term = lax.dot_general(
                lhs[0:at, :], y_ref[...], (((1,), (1,)), ((), ())), preferred_element_type=F32
            )
            total = term if total is None else total + term
        at = 0
        for k, tap, first, count, row, begin, end in rows:
            got = total[at + first - begin : at + first - begin + count]
            at += end - begin
            where = slice(row, row + count)
            if accumulate:
                low[k, where, :] += got[:, :128]
                high[k, where, 0:64] += got[:, 128:]
            else:
                low[k, where, :] = got[:, :128]
                high[k, where, 0:64] = got[:, 128:]


def at_place(run):
    _, _, mine, line = place()
    for place4 in range(4):
        for r in range(2):
            pl.when((mine == place4) & ((line & 1) == r))(functools.partial(run, place4, r))


def pairs_for(own, swap, far, even):
    (xo, yo), (xs, ys), (xf, yf) = own, swap, far
    lower, upper = ((xo, yo), (xs, ys)) if even else ((xs, ys), (xo, yo))
    near = ([(lower[0], upper[1])], [lower, upper], [(upper[0], lower[1])])
    first, last = [(xf, yo)], [(xo, yf)]
    return near, (first if even else last, [], last if even else first)


def near_body(xo, xop, yo, yop, xs, xsp, ys, ysp, low, high, *rest):
    fulls, lhs = rest[0:4], rest[4]
    half, _, _, line = place()
    for full, parts in zip(fulls, ((xo, xop), (yo, yop), (xs, xsp), (ys, ysp))):
        fill(full, parts, half, 0)

    def run(place4, r):
        near, _ = pairs_for(fulls[0:2], fulls[2:4], (None, None), place4 < 2)
        products(place4, r, lambda a: near[a], False, [(line >> 1) ^ 1], lhs, low, high, xo.shape[1])

    at_place(run)


def emit(low, high, row, norm, out, plain=False):
    count = low.shape[1] // 2
    if plain:
        by = norm
    else:
        top = jnp.maximum(jnp.max(jnp.abs(low[row])), jnp.max(jnp.abs(high[row, :, 0:64])))
        top = jnp.maximum(jnp.broadcast_to(top, (8, 128)) * norm, 1e-25)
        power = jnp.floor(jnp.log(TOP / top) * (1.0 / math.log(2.0)))
        out[3 * count : 3 * count + 2, :] = power[0:2]
        by = jnp.exp2(power)[0:1] * norm
    left = lax.broadcasted_iota(jnp.int32, (count, 128), 1) < 64
    even_low = low[row, pl.ds(0, count, stride=2), :]
    odd_low = pltpu.roll(low[row, pl.ds(1, count, stride=2), :], 64, 1)
    even_high = high[row, pl.ds(0, count, stride=2), :]
    odd_high = pltpu.roll(high[row, pl.ds(1, count, stride=2), :], 64, 1)
    out[pl.ds(0, count, stride=3), :] = even_low * by
    out[pl.ds(1, count, stride=3), :] = jnp.where(left, even_high, odd_low) * by
    out[pl.ds(2, count, stride=3), :] = jnp.where(left, odd_low, odd_high) * by


def far_body(norm, low_in, high_in, xof, yof, xr, xrp, yr, yrp, out_ref, xrf, yrf, lhs, low, high):
    half, _, _, line = place()
    fill(xrf, (xr, xrp), half, 0, relay=True)
    fill(yrf, (yr, yrp), half, 0, relay=True)
    low[...] = low_in[...]
    high[...] = high_in[...]

    def run(place4, r):
        _, far = pairs_for((xof, yof), (None, None), (xrf, yrf), place4 < 2)
        products(place4, r, lambda a: far[a], True, [(line >> 1) ^ 1], lhs, low, high, xr.shape[1])

    at_place(run)
    emit(low, high, 0, norm, out_ref)


def rest_body(step, norm, *refs):
    fulls, (out_ref, lhs, low, high) = refs[0:6], refs[6:]
    _, _, _, line = place()
    in_half = fulls[0].shape[0] // 2

    def run(place4, r):
        near, far = pairs_for(fulls[0:2], fulls[2:4], fulls[4:6], place4 < 2)
        halves = [(line >> 1) ^ (step >> 1)]
        chosen = r ^ (step & 1)
        products(place4, chosen, lambda a: near[a] + far[a], False, halves, lhs, low, high, in_half)

    at_place(run)
    emit(low, high, 0, norm, out_ref, plain=step == 0)


def split_gradient(own, swap, relay, norm, later):
    own, swap, relay = ((x, xp, y, yp) for x, xp, y, yp in (own, swap, relay))
    _, in_half, size = own[0].shape
    out_half = own[2].shape[1]
    rows = 27 * in_half // CHUNKS
    flat = rows * 3 // 2
    part = jax.ShapeDtypeStruct((1, rows, 128), F32)
    sent = jax.ShapeDtypeStruct((flat + 2, 128), F32)
    mine = jax.ShapeDtypeStruct((flat, 128), F32)
    whole = [jax.ShapeDtypeStruct((2 * half, size), BF16) for half in (in_half, out_half)]
    lhs = pltpu.VMEM((1024, size), BF16)
    work = rows * 2 * out_half * 2 * size

    sums = [pltpu.VMEM(part.shape, F32)] * 2
    low, high, *near = call(
        near_body, [part, part, *whole, *whole], [*own, *swap], [lhs], 4 * work // 3, "near"
    )
    term, *far = call(
        functools.partial(far_body, norm),
        [sent, *whole],
        [low, high, *near[0:2], *relay],
        [lhs, *sums],
        2 * work // 3,
        "far",
    )
    term, gots, first = term.astype(jnp.float16), [], near[0]

    def rest(step, shape):
        body = functools.partial(rest_body, step, norm)
        return call(body, [shape], [first, *near[1:], *far], [lhs, *sums], 2 * work, "rest")[0]

    for step, following in ((2, 1), (1, 3)):
        term, first = lax.optimization_barrier((term, first))
        gots.append(swapped(term, 4 * step))
        term = rest(following, sent).astype(jnp.float16)
    gots.append(swapped(term, 12))
    later, first = lax.optimization_barrier((later, first))
    kept = rest(0, mine)
    out = jax.ShapeDtypeStruct((flat, 1, 128), F32)
    operands = [kept, *(got.astype(F32) for got in gots)]
    return call(sum_body, [out], operands, [], 0, "sum")[0].reshape(1, flat * 128), later


def sum_body(own, *refs):
    gots, out_ref = refs[:-1], refs[-1]
    flat = own.shape[0]
    total = own[...]
    for got in gots:
        total = total + got[0:flat, :] * jnp.exp2(-got[flat : flat + 1, :])
    out_ref[:, 0, :] = total


def any_gradient(own, swap, relay, norm):
    count = lax.axis_size(AXIS)
    half, odd, _, _ = place()

    def whole(mine, other):
        parts = jnp.concatenate([mine, other], axis=1), jnp.concatenate([other, mine], axis=1)
        return jnp.where(half == 0, *parts)

    near, next_to, far = (whole(p[0], p[1]) for p in (own, swap, relay))
    cotangent = whole(own[2], own[3])[0]
    in_half, size = own[0].shape[1:]
    far = jnp.where(at_edge(), jnp.zeros_like(far), far)
    planes = [jnp.where(odd == 0, far, next_to), near, jnp.where(odd == 0, next_to, far)]
    column = jnp.arange(size, dtype=jnp.int32) % W
    found = []
    for plane in planes:
        mine = lax.dynamic_slice_in_dim(plane[0], half * in_half, in_half, 0)
        margin = jnp.pad(mine, [(0, 0), (W + 1, W + 1)])
        for b in range(3):
            for e in range(3):
                start = W * b + e
                here = (column + e - 1 >= 0) & (column + e - 1 < W)
                shifted = jnp.where(here, margin[:, start : start + size], jnp.zeros((), mine.dtype))
                found.append(jnp.einsum("kp,op->ko", shifted, cotangent, preferred_element_type=F32))
    term = jnp.stack(found).reshape(1, -1) * norm
    both = jnp.concatenate([jnp.where(half == 0, term, 0.0), jnp.where(half == 0, 0.0, term)])
    return lax.psum_scatter(both.reshape(count, -1), AXIS, scatter_dimension=0, tiled=True)


def local(activations, weights, cotangent):
    count = lax.axis_size(AXIS)
    size = activations.shape[2]
    next_x = swapped(activations, 2)
    own_x, own_y = staged(activations, cotangent)
    next_y = swapped(own_y, 2)
    later_y, near_x = lax.optimization_barrier((own_y, next_x))
    far_x, far_y = relayed(near_x), handed(later_y)
    other_x = swapped(own_x, 1)
    tables = weight_tables(weights)
    later_own, tables = lax.optimization_barrier((own_y, tables))
    other_y = swapped(later_own, 1)
    next_other_x, next_other_y = swapped(next_x, 1), swapped(next_y, 1)
    far_other_x, far_other_y = swapped(far_x, 1), swapped(far_y, 1)
    own = (own_x, other_x, own_y, other_y)
    swap = (next_x, next_other_x, next_y, next_other_y)
    relay = (far_x, far_other_x, far_y, far_other_y)
    norm = 1.0 / math.sqrt(count // 2 * size)
    fits = count == 16 and activations.shape[1] == 96 and cotangent.shape[1] == 96
    xs = [part for plane in (own, swap, relay) for part in plane[:2]]
    ys = [part for plane in (own, swap, relay) for part in plane[2:]]
    forward, back = convolutions(xs, ys, tables)
    if fits:
        gradient, forward = split_gradient(own, swap, relay, norm, forward)
    else:
        gradient = any_gradient(own, swap, relay, norm)
    return forward, back, gradient


def solution(mesh):
    placed = P(("grp", AXIS), None, None)
    return jax.shard_map(
        local,
        mesh=mesh,
        in_specs=(placed, P(), placed),
        out_specs=(placed, placed, P(("grp", AXIS), None)),
        check_vma=False,
    )
```
